128 devices in a mesh: gx: 8 (over z, y_lo), gy: 4 (over y_hi, core), gz: 4 (over x).
Axes of the slice: x: 4, y: 4 (y_hi: 2, y_lo: 2; y = y_hi * 2 + y_lo), z: 4, core: 2. Of those that a mesh axis runs over, the one named last changes fastest.
Arguments:
- residual: float32 [64, 3, 32, 16, 512], P(None, None, 'gx', 'gy', 'gz'), may hold values from -8 to 8
- interface_scaling: float32 [3, 32, 16, 512], P(None, 'gx', 'gy', 'gz'), may hold values from 0.3 to 0.7
- primal_basis: bfloat16 [8, 4, 4, 128, 6144], P('gx', 'gy', 'gz'), may hold values from -0.078125 to 0.078125
- primal_index: int32 [8, 4, 4, 128], P('gx', 'gy', 'gz'), may hold values from 0 to 1023
- coarse_inverse: float32 [8192, 1024], P('gx'), may hold values from -2 to 2
- schur_tiles: bfloat16 [8, 4, 4, 48, 6, 128, 128], P('gx', 'gy', 'gz'), may hold values from -0.3125 to 0.3125
- tile_cols: int32 [8, 4, 4, 48, 6], P('gx', 'gy', 'gz'), may hold values from 0 to 47
- tile_count: int32 [8, 4, 4, 48], P('gx', 'gy', 'gz'), may hold values from 1 to 6, as said below
- region_id: int32 [8, 4, 4], P('gx', 'gy', 'gz'), may hold values from 0 to 7
- region_viscosity: float32 [8], replicated, may hold values from 0.5 to 4
Outputs:
- preconditioned: float32 [64, 3, 32, 16, 512], P(None, None, 'gx', 'gy', 'gz')
The draws below stay inside these ranges and needn't reach their ends.
Inputs may be any that keep to these rules, and one draw needn't show every extreme that they name: Only the first tile_count slots of a block row carry tiles; some block row has all 6 in every draw.
All inputs are finite; a program needn't handle non-finite values.
Results may differ from the reference program's by a relative error of at most 0.004.
Values sent between devices are 32-bit elements; how exact they have to be, the bound alone decides.
A program may use at most 128 MiB of HBM per device.

```python
import math
import jax
import jax.numpy as jnp
from jax import lax

RHS = 64
COMPONENTS = 3
CX = 4
CY = 4
CZ = 128
TILE_SLOTS = 6
PRIMAL = 128
COARSE = 1024
REGIONS = 8
BLOCKS = 48
LOCAL_LEN = 6144
NX = 32
NY = 16
NZ = 512
COARSE_ROWS = 8192
N_GX = 8
N_GY = 4
N_GZ = 4


def draw_coarse_inverse(key, part):
    diag_key = jax.random.fold_in(key, 11)
    off_key = jax.random.fold_in(key, 12)
    row_ids = jnp.arange(COARSE_ROWS)[:, None] % COARSE
    col_ids = jnp.arange(COARSE)[None, :]
    diagonal = jax.random.uniform(diag_key, (COARSE_ROWS, 1), jnp.float32, 1.0, 2.0)
    off_part = jax.random.normal(off_key, (COARSE_ROWS, COARSE), jnp.float32) * (0.6 / math.sqrt(COARSE))
    return jnp.where(row_ids == col_ids, diagonal, off_part).astype(jnp.float32)


def draw_tile_count(key, part):
    light_key = jax.random.fold_in(key, 21)
    heavy_key = jax.random.fold_in(key, 22)
    extra_key = jax.random.fold_in(key, 23)
    shape_all = (N_GX, N_GY, N_GZ, BLOCKS)
    light = jax.random.randint(light_key, shape_all, 1, max(2, TILE_SLOTS // 3) + 1)
    heavy_device = jax.random.randint(heavy_key, (N_GX, N_GY, N_GZ, 1), 0, 6) == 0
    heavy = jax.random.randint(extra_key, shape_all, max(1, TILE_SLOTS // 2), TILE_SLOTS + 1)
    counts = jnp.where(heavy_device, heavy, light)
    counts = counts.at[0, 0, 0, 0].set(TILE_SLOTS)
    return counts.astype(jnp.int32)


def plant(values, key, least, top_value):
    dims = values.shape
    spot = [jax.random.randint(jax.random.fold_in(key, axis), (), 0, dims[axis]) for axis in range(len(dims))]
    values = values.at[tuple(spot)].set(least)
    longest = dims.index(max(dims))
    spot[longest] = (spot[longest] + 1) % dims[longest]
    return values.at[tuple(spot)].set(top_value)


def shard_levels(own_key, dims, split, low, largest):
    def one(axis_at, parts):
        steps = jax.random.uniform(jax.random.fold_in(jax.random.fold_in(own_key, 6), axis_at), (parts,), jnp.float32, low / len(split), largest / len(split))
        return jnp.repeat(jnp.exp(steps), dims[axis_at] // parts).reshape((-1,) + (1,) * (len(dims) - axis_at - 1))

    level = one(*split[0])
    for cut in split[1:]:
        level = level * one(*cut)
    return level


def gaussian(own_key, shape, spread, reach, shards=(), kind=jnp.bfloat16):
    entries = spread * jax.random.normal(own_key, shape, jnp.float32)
    if shards:
        entries = entries * shard_levels(own_key, shape, shards, -0.22, 0.18)
    return jnp.clip(entries, -reach, reach).astype(kind)


def setup_inputs(seed: int = 0) -> dict:
    arg_keys = jax.random.split(jax.random.key(seed), 11)
    residual = gaussian(arg_keys[0], (RHS, COMPONENTS, NX, NY, NZ), 1.0, 8.0, ((2, 8), (3, 4), (4, 4)), jnp.float32)
    interface_scaling = jnp.clip(0.3 + 0.39999998 * jax.random.uniform(arg_keys[1], (COMPONENTS, NX, NY, NZ), jnp.float32) ** shard_levels(arg_keys[1], (COMPONENTS, NX, NY, NZ), ((1, 8), (2, 4), (3, 4)), -0.2, 0.2), 0.3, 0.7)
    primal_basis = gaussian(arg_keys[2], (N_GX, N_GY, N_GZ, PRIMAL, LOCAL_LEN), LOCAL_LEN ** -0.5, 0.078125, ((0, 8), (1, 4), (2, 4)))
    primal_index = plant(jax.random.randint(arg_keys[3], (N_GX, N_GY, N_GZ, PRIMAL), 0, COARSE), jax.random.fold_in(arg_keys[3], 1), 0, COARSE - 1).astype(jnp.int32)
    coarse_inverse = draw_coarse_inverse(jax.random.fold_in(arg_keys[10], 71), 0)
    schur_tiles = gaussian(arg_keys[5], (N_GX, N_GY, N_GZ, BLOCKS, TILE_SLOTS, CZ, CZ), (3 * CZ) ** -0.5, 0.3125, ((0, 8), (1, 4), (2, 4)))
    tile_cols = plant(jax.random.randint(arg_keys[6], (N_GX, N_GY, N_GZ, BLOCKS, TILE_SLOTS), 0, BLOCKS), jax.random.fold_in(arg_keys[6], 1), 0, BLOCKS - 1).astype(jnp.int32)
    tile_count = draw_tile_count(jax.random.fold_in(arg_keys[10], 71), 0)
    region_id = plant(jax.random.randint(arg_keys[8], (N_GX, N_GY, N_GZ), 0, REGIONS), jax.random.fold_in(arg_keys[8], 1), 0, REGIONS - 1).astype(jnp.int32)
    region_viscosity = jnp.clip(jnp.exp(jax.random.uniform(arg_keys[9], (REGIONS,), jnp.float32, math.log(0.5), math.log(4.0))), 0.5, 4.0)
    return {"residual": residual, "interface_scaling": interface_scaling, "primal_basis": primal_basis, "primal_index": primal_index, "coarse_inverse": coarse_inverse, "schur_tiles": schur_tiles, "tile_cols": tile_cols, "tile_count": tile_count, "region_id": region_id, "region_viscosity": region_viscosity}


def interface_sum(grid_field):
    summed = grid_field
    for axis_id, block_len in ((2, CX), (3, CY), (4, CZ)):
        extent = grid_field.shape[axis_id]
        padded = jnp.pad(grid_field, [(1, 1) if dim_id == axis_id else (0, 0) for dim_id in range(5)])
        below = lax.slice_in_dim(padded, 0, extent, axis=axis_id)
        above = lax.slice_in_dim(padded, 2, extent + 2, axis=axis_id)
        positions = jnp.arange(extent)
        mask_shape = [extent if dim_id == axis_id else 1 for dim_id in range(5)]
        at_start = ((positions % block_len == 0) & (positions > 0)).reshape(mask_shape)
        at_end = ((positions % block_len == block_len - 1) & (positions < extent - 1)).reshape(mask_shape)
        summed = summed + jnp.where(at_start, below, 0.0) + jnp.where(at_end, above, 0.0)
    return summed

def to_subdomains(grid_values):
    blocked = grid_values.reshape(RHS, COMPONENTS, N_GX, CX, N_GY, CY, N_GZ, CZ)
    moved = blocked.transpose(2, 4, 6, 0, 1, 3, 5, 7)
    return moved.reshape(N_GX * N_GY * N_GZ, RHS, LOCAL_LEN)

def from_subdomains(local_values):
    blocked = local_values.reshape(N_GX, N_GY, N_GZ, RHS, COMPONENTS, CX, CY, CZ)
    moved = blocked.transpose(3, 4, 0, 5, 1, 6, 2, 7)
    return moved.reshape(RHS, COMPONENTS, NX, NY, NZ)

def make_one_hot(indices):
    return (indices[:, None] == jnp.arange(COARSE)[None, :]).astype(jnp.float32)

def reference(residual, interface_scaling, primal_basis, primal_index, coarse_inverse, schur_tiles, tile_cols, tile_count, region_id, region_viscosity):
    highest = lax.Precision.HIGHEST
    weighted = (interface_scaling[None] * interface_sum(residual)).astype(jnp.bfloat16)
    subdomains = to_subdomains(weighted)
    count_all = N_GX * N_GY * N_GZ
    basis_all = primal_basis.reshape(count_all, PRIMAL, LOCAL_LEN)
    index_all = primal_index.reshape(count_all, PRIMAL)

    def restrict(inputs):
        rows, basis, indices = inputs
        coarse_part = lax.dot_general(rows, basis, (((1,), (1,)), ((), ())), preferred_element_type=jnp.float32)
        return jnp.dot(coarse_part, make_one_hot(indices), precision=highest)
    contributions = lax.map(restrict, (subdomains, basis_all, index_all))
    group_sums = lax.optimization_barrier(jnp.sum(contributions.reshape(N_GX, N_GY * N_GZ, RHS, COARSE), axis=1))
    inverse_blocks = coarse_inverse.reshape(N_GX, COARSE, COARSE)
    solutions = jnp.einsum('grn,gmn->grm', group_sums, inverse_blocks, precision=highest)
    groups = (jnp.arange(count_all) // (N_GY * N_GZ)).astype(jnp.int32)
    tiles_all = schur_tiles.reshape(count_all, BLOCKS, TILE_SLOTS, CZ, CZ)
    cols_all = tile_cols.reshape(count_all, BLOCKS, TILE_SLOTS)
    live_all = tile_count.reshape(count_all, BLOCKS)
    region_all = region_id.reshape(count_all)
    scale_factor = math.sqrt(LOCAL_LEN / PRIMAL)

    def correct(inputs):
        rows, basis, indices, tiles, columns, live, region_now, group_now = inputs
        picked = jnp.dot(solutions[group_now], make_one_hot(indices).T, precision=highest).astype(jnp.bfloat16)
        coarse_fix = jnp.dot(picked, basis, preferred_element_type=jnp.float32) * scale_factor
        blocks = rows.reshape(RHS, BLOCKS, CZ)
        schur_sum = jnp.zeros((RHS, BLOCKS, CZ), jnp.float32)
        for slot in range(TILE_SLOTS):
            chosen = jnp.take(blocks, columns[:, slot], axis=1).astype(jnp.float32)
            product = jnp.einsum('bij,sbj->sbi', tiles[:, slot].astype(jnp.float32), chosen, precision=highest)
            schur_sum = schur_sum + jnp.where((live > slot)[None, :, None], product, 0.0)
        inverse_visc = jnp.sum(jnp.where(jnp.arange(REGIONS) == region_now, 1.0 / region_viscosity, 0.0))
        return coarse_fix + schur_sum.reshape(RHS, LOCAL_LEN) * inverse_visc
    corrections = lax.map(correct, (subdomains, basis_all, index_all, tiles_all, cols_all, live_all, region_all, groups))
    correction = from_subdomains(corrections)
    return interface_scaling[None] * interface_sum(correction)
```

```python
import functools
import math

import jax
import jax.numpy as jnp
from jax import lax
from jax.experimental import pallas as pl
from jax.experimental.pallas import tpu as pltpu
from jax.sharding import PartitionSpec as P

MESH = pl.DeviceIdType.MESH
CHUNKS = 2
GROUP_Y = 4
GROUP_Z = 4
SLOTS = GROUP_Y * GROUP_Z
NEAR = tuple((a, b) for a in range(2) for b in range(GROUP_Z) if (a, b) != (0, 0))
FULL = tuple((a, b) for a in range(GROUP_Y) for b in range(GROUP_Z) if (a, b) != (0, 0))
BF16 = jnp.bfloat16
F32 = jnp.float32
NT = (((1,), (1,)), ((), ()))


def flipped(gy, a):
    return (gy, gy + 1 - 2 * (gy % 2), (gy + 2) % 4, 3 - gy)[a]


def kernel(
    sizes,
    res_hbm,
    scale_hbm,
    basis_hbm,
    index_smem,
    index_hbm,
    inverse_hbm,
    tiles_hbm,
    cols_smem,
    count_smem,
    region_smem,
    visc_smem,
    out_hbm,
    lin,
    scale,
    basis,
    inverse,
    tiles,
    index_all,
    field,
    weighted,
    corr,
    zpack,
    x_low,
    x_high,
    y_low,
    y_high,
    z_low,
    z_high,
    parts,
    part_own,
    picked_rows,
    split_rows,
    gathered,
    load_sem,
    in_sem,
    out_sem,
    face_send,
    face_recv,
    index_send,
    index_recv,
    part_send,
    part_recv,
):
    n_gx, n_gy, n_gz, rhs, blocks, comps, slots = sizes
    rows = rhs // CHUNKS
    gx, gy, gz = lax.axis_index("gx"), lax.axis_index("gy"), lax.axis_index("gz")

    sides = (
        (gx > 0, (gx - 1, gy, gz)),
        (gx < n_gx - 1, (gx + 1, gy, gz)),
        (gy > 0, (gx, gy - 1, gz)),
        (gy < n_gy - 1, (gx, gy + 1, gz)),
        (gz > 0, (gx, gy, gz - 1)),
        (gz < n_gz - 1, (gx, gy, gz + 1)),
    )

    def peer(a, b):
        return (gx, flipped(gy, a), (gz + b) % GROUP_Z)

    def load_chunk(c):
        span = pl.ds(c * rows * blocks, rows * blocks)
        return pltpu.make_async_copy(res_hbm.at[span], lin.at[span], in_sem.at[c])

    loads = (
        pltpu.make_async_copy(index_hbm, index_all.at[0], load_sem.at[0]),
        pltpu.make_async_copy(scale_hbm, scale, load_sem.at[1]),
        pltpu.make_async_copy(inverse_hbm, inverse, load_sem.at[2]),
        pltpu.make_async_copy(basis_hbm, basis, load_sem.at[3]),
        pltpu.make_async_copy(tiles_hbm, tiles, load_sem.at[4]),
    )
    for c in range(CHUNKS):
        load_chunk(c).start()
    for copy in loads:
        copy.start()

    barrier = pltpu.get_barrier_semaphore()
    expected = 0
    for there, device in sides:

        @pl.when(there)
        def _():
            pl.semaphore_signal(barrier, inc=1, device_id=device, device_id_type=MESH)

        expected = expected + there.astype(jnp.int32)
    for a, b in FULL:
        pl.semaphore_signal(barrier, inc=1, device_id=peer(a, b), device_id_type=MESH)
    pl.semaphore_wait(barrier, expected + len(FULL))

    loads[0].wait()

    def index_copy(a, b):
        k = a * GROUP_Z + b
        return pltpu.make_async_remote_copy(
            src_ref=index_all.at[0],
            dst_ref=index_all.at[k],
            send_sem=index_send.at[k],
            recv_sem=index_recv.at[k],
            device_id=peer(a, b),
            device_id_type=MESH,
        )

    for a, b in FULL:
        index_copy(a, b).start()

    lane = lax.broadcasted_iota(jnp.int32, (rows, 128), 1)

    def face_copies(phase, source, c):
        pairs = (
            (source.at[c, :, 0], x_high),
            (source.at[c, :, 3], x_low),
            (source.at[c, :, :, 0], y_high),
            (source.at[c, :, :, 3], y_low),
            (zpack.at[phase, c], z_high),
            (zpack.at[phase, c], z_low),
        )
        return [
            pltpu.make_async_remote_copy(
                src_ref=src,
                dst_ref=dst.at[phase, c],
                send_sem=face_send.at[phase, c, side],
                recv_sem=face_recv.at[phase, c, side ^ 1],
                device_id=sides[side][1],
                device_id_type=MESH,
            )
            for side, (src, dst) in enumerate(pairs)
        ]

    landing = (x_low, x_high, y_low, y_high, z_low, z_high)

    def send_faces(phase, source, c):
        for side, copy in enumerate(face_copies(phase, source, c)):

            @pl.when(sides[side][0])
            def _():
                copy.start()

    def await_faces(phase, source, c):
        for side, copy in enumerate(face_copies(phase, source, c)):
            land = landing[side].at[phase, c]
            arrived = pltpu.make_async_remote_copy(
                src_ref=land,
                dst_ref=land,
                send_sem=face_send.at[phase, c, side],
                recv_sem=face_recv.at[phase, c, side],
                device_id=sides[side][1],
                device_id_type=MESH,
            )

            @pl.when(sides[side][0])
            def _():
                arrived.wait_recv()

    def drain_faces(phase, source, c):
        for side, copy in enumerate(face_copies(phase, source, c)):

            @pl.when(sides[side][0])
            def _():
                copy.wait_send()

    for side in range(6):

        @pl.when(jnp.logical_not(sides[side][0]))
        def _():
            landing[side][...] = jnp.zeros_like(landing[side])

    def packed(acc, value, b):
        return jnp.where(lane // 2 == b, pltpu.roll(value, 2 * b + 1, 1), acc)

    def pack_first(c):
        def body(comp, acc):
            for x in range(4):
                for y in range(4):
                    b = comp * 16 + x * 4 + y
                    value = lin[pl.ds(c * rows * blocks + b, rows, stride=blocks), :]
                    field[c, comp, x, y] = value
                    acc = packed(acc, value, b)
            return acc

        zpack[0, c] = lax.fori_loop(0, comps, body, jnp.zeros((rows, 128), F32))

    def interface_sum(phase, source, c, emit):
        low = pltpu.roll(z_low[phase, c], 1, 1)
        high = pltpu.roll(z_high[phase, c], 127, 1)
        ends = jnp.where(lane % 2 == 1, low, high)
        edge = (lane == 0) | (lane == 127)

        def body(comp, carry):
            for x in range(4):
                for y in range(4):
                    b = comp * 16 + x * 4 + y
                    total = source[c, comp, x, y]
                    total = total + jnp.where(edge, pltpu.roll(ends, 127 - 2 * b, 1), 0.0)
                    if x == 0:
                        total = total + x_low[phase, c, comp, y]
                    if x == 3:
                        total = total + x_high[phase, c, comp, y]
                    if y == 0:
                        total = total + y_low[phase, c, comp, x]
                    if y == 3:
                        total = total + y_high[phase, c, comp, x]
                    emit(b, total * scale[pl.ds(b, 1), :])
            return carry

        lax.fori_loop(0, comps, body, 0)

    for c in range(CHUNKS):
        load_chunk(c).wait()
        pack_first(c)
        send_faces(0, field, c)

    loads[2].wait()

    def pick_row(p, carry):
        picked_rows[pl.ds(p, 1), :] = inverse[pl.ds(index_smem[p], 1), :]
        return carry

    lax.fori_loop(0, 128, pick_row, 0, unroll=8)
    rows_f32 = picked_rows[...]
    high_part = rows_f32.astype(BF16)
    split_rows[0:128, :] = high_part
    split_rows[128:256, :] = (rows_f32 - high_part.astype(F32)).astype(BF16)

    for a, b in FULL:
        index_copy(a, b).wait_recv()

    def pick_columns(k, carry):
        coarse = split_rows.shape[1]
        ids = lax.broadcasted_iota(jnp.int32, (coarse, 128), 0)
        one_hot = jnp.where(ids == index_all[k], 1.0, 0.0).astype(BF16)
        found = jnp.dot(split_rows[...], one_hot, preferred_element_type=F32).astype(BF16)
        gathered[k] = found
        return carry

    lax.fori_loop(0, SLOTS, pick_columns, 0)

    def part_copy(c, a, b, forward):
        slot = (a + 2) * GROUP_Z + b if forward else a * GROUP_Z + b
        return pltpu.make_async_remote_copy(
            src_ref=parts.at[c, 2 * GROUP_Z] if forward else part_own.at[c],
            dst_ref=parts.at[c, slot],
            send_sem=part_send.at[c, slot],
            recv_sem=part_recv.at[c, slot],
            device_id=peer(a, b),
            device_id_type=MESH,
        )

    loads[1].wait()
    loads[3].wait()
    visc = jnp.full((rows, 128), visc_smem[region_smem[0]], F32)
    inv_visc = 1.0 / visc
    coarse_scale = math.sqrt(blocks * 128 / 128)

    for c in range(CHUNKS):
        await_faces(0, field, c)

        def keep(b, value):
            weighted[c, b] = value.astype(BF16)

        interface_sum(0, field, c, keep)
        weighted[c, blocks] = jnp.zeros((rows, 128), BF16)

        def restrict(comp, acc):
            lhs = jnp.concatenate([weighted[c, comp * 16 + j] for j in range(16)], axis=1)
            rhs_part = basis[:, pl.ds(pl.multiple_of(comp * 2048, 2048), 2048)]
            return acc + lax.dot_general(lhs, rhs_part, NT, preferred_element_type=F32)

        part = lax.fori_loop(0, comps, restrict, jnp.zeros((rows, 128), F32))
        part_own[c] = part
        parts[c, 0] = part
        part_copy(c, 2, 0, False).start()
        for a, b in NEAR:
            part_copy(c, a, b, False).start()

        if c == 0:
            loads[4].wait()

        def schur_row(r, carry):
            picks = [
                weighted[c, jnp.where(k < count_smem[r], cols_smem[r * slots + k], blocks)]
                for k in range(slots)
            ]
            lhs = jnp.concatenate(picks, axis=1)
            tile = jnp.concatenate([tiles[r, k] for k in range(slots)], axis=1)
            product = lax.dot_general(lhs, tile, NT, preferred_element_type=F32)
            corr[c, r // 16, (r // 4) % 4, r % 4] = product * inv_visc
            return carry

        lax.fori_loop(0, 12, schur_row, 0, unroll=2)
        part_copy(c, 2, 0, False).wait_recv()
        for a, b in NEAR:
            part_copy(c, a, b, True).start()
        lax.fori_loop(12, blocks, schur_row, 0, unroll=2)
        for a, b in NEAR:
            part_copy(c, a, b, False).wait_recv()
            part_copy(c, a, b, True).wait_recv()

        everyone = jnp.concatenate([parts[c, k] for k in range(SLOTS)], axis=1)
        top = everyone.astype(BF16)
        rest = (everyone - top.astype(F32)).astype(BF16)
        inv_high = jnp.concatenate([gathered[k, 0:128] for k in range(SLOTS)], axis=1)
        inv_low = jnp.concatenate([gathered[k, 128:256] for k in range(SLOTS)], axis=1)
        local = lax.dot_general(top, inv_high, NT, preferred_element_type=F32)
        local = local + lax.dot_general(rest, inv_high, NT, preferred_element_type=F32)
        local = local + lax.dot_general(top, inv_low, NT, preferred_element_type=F32)
        local = local.astype(BF16)

        def prolong(comp, acc):
            rhs_part = basis[:, pl.ds(pl.multiple_of(comp * 2048, 2048), 2048)]
            fix = jnp.dot(local, rhs_part, preferred_element_type=F32) * coarse_scale
            for x in range(4):
                for y in range(4):
                    j = x * 4 + y
                    value = corr[c, comp, x, y] + fix[:, j * 128 : (j + 1) * 128]
                    corr[c, comp, x, y] = value
                    acc = packed(acc, value, comp * 16 + j)
            return acc

        zpack[1, c] = lax.fori_loop(0, comps, prolong, jnp.zeros((rows, 128), F32))
        send_faces(1, corr, c)

    def store_chunk(c):
        span = pl.ds(c * rows * blocks, rows * blocks)
        return pltpu.make_async_copy(lin.at[span], out_hbm.at[span], out_sem.at[c])

    for c in range(CHUNKS):
        await_faces(1, corr, c)

        def emit(b, value):
            lin[pl.ds(c * rows * blocks + b, rows, stride=blocks), :] = value

        interface_sum(1, corr, c, emit)
        store_chunk(c).start()

    for c in range(CHUNKS):
        drain_faces(0, field, c)
        drain_faces(1, corr, c)
        part_copy(c, 2, 0, False).wait_send()
        for a, b in NEAR:
            part_copy(c, a, b, False).wait_send()
            part_copy(c, a, b, True).wait_send()
        store_chunk(c).wait()
    for a, b in FULL:
        index_copy(a, b).wait_send()


def per_device(
    residual,
    interface_scaling,
    primal_basis,
    primal_index,
    coarse_inverse,
    schur_tiles,
    tile_cols,
    tile_count,
    region_id,
    region_viscosity,
):
    rhs, comps, cells_x, cells_y, cells_z = residual.shape
    blocks = comps * cells_x * cells_y
    slots = schur_tiles.shape[4]
    primal = primal_basis.shape[3]
    coarse = coarse_inverse.shape[1]
    rows = rhs // CHUNKS
    sizes = (
        lax.axis_size("gx"),
        lax.axis_size("gy"),
        lax.axis_size("gz"),
        rhs,
        blocks,
        comps,
        slots,
    )
    face = pltpu.VMEM((2, CHUNKS, comps, cells_x, rows, cells_z), F32)
    ends = pltpu.VMEM((2, CHUNKS, rows, cells_z), F32)
    dma = pltpu.SemaphoreType.DMA
    hbm = pl.BlockSpec(memory_space=pl.ANY)
    smem = pl.BlockSpec(memory_space=pltpu.SMEM)
    out = pl.pallas_call(
        functools.partial(kernel, sizes),
        out_shape=jax.ShapeDtypeStruct((rhs * blocks, cells_z), F32),
        in_specs=[hbm, hbm, hbm, smem, hbm, hbm, hbm, smem, smem, smem, smem],
        out_specs=hbm,
        scratch_shapes=[
            pltpu.VMEM((rhs * blocks, cells_z), F32),
            pltpu.VMEM((blocks, cells_z), F32),
            pltpu.VMEM((primal, blocks * cells_z), BF16),
            pltpu.VMEM((coarse, coarse), F32),
            pltpu.VMEM((blocks, slots, cells_z, cells_z), BF16),
            pltpu.VMEM((SLOTS, 1, primal), jnp.int32),
            pltpu.VMEM((CHUNKS, comps, cells_x, cells_y, rows, cells_z), F32),
            pltpu.VMEM((CHUNKS, blocks + 1, rows, cells_z), BF16),
            pltpu.VMEM((CHUNKS, comps, cells_x, cells_y, rows, cells_z), F32),
            ends,
            face,
            face,
            face,
            face,
            ends,
            ends,
            pltpu.VMEM((CHUNKS, SLOTS, rows, primal), F32),
            pltpu.VMEM((CHUNKS, rows, primal), F32),
            pltpu.VMEM((primal, coarse), F32),
            pltpu.VMEM((2 * primal, coarse), BF16),
            pltpu.VMEM((SLOTS, 2 * primal, primal), BF16),
            dma((5,)),
            dma((CHUNKS,)),
            dma((CHUNKS,)),
            dma((2, CHUNKS, 6)),
            dma((2, CHUNKS, 6)),
            dma((SLOTS,)),
            dma((SLOTS,)),
            dma((CHUNKS, SLOTS)),
            dma((CHUNKS, SLOTS)),
        ],
        compiler_params=pltpu.CompilerParams(
            collective_id=0, has_side_effects=True, vmem_limit_bytes=52 * 2**20
        ),
    )(
        residual.reshape(rhs * blocks, cells_z),
        interface_scaling.reshape(blocks, cells_z),
        primal_basis.reshape(primal, blocks * cells_z),
        primal_index.reshape(primal),
        primal_index.reshape(1, primal),
        coarse_inverse,
        schur_tiles.reshape(blocks, slots, cells_z, cells_z),
        tile_cols.reshape(blocks * slots),
        tile_count.reshape(blocks),
        region_id.reshape(1),
        region_viscosity,
    )
    return out.reshape(residual.shape)


def solution(mesh):
    in_specs = (
        P(None, None, "gx", "gy", "gz"),
        P(None, "gx", "gy", "gz"),
        P("gx", "gy", "gz", None, None),
        P("gx", "gy", "gz", None),
        P("gx", None),
        P("gx", "gy", "gz", None, None, None, None),
        P("gx", "gy", "gz", None, None),
        P("gx", "gy", "gz", None),
        P("gx", "gy", "gz"),
        P(),
    )
    out_specs = P(None, None, "gx", "gy", "gz")
    return jax.shard_map(
        per_device, mesh=mesh, in_specs=in_specs, out_specs=out_specs, check_vma=False
    )
```

```python
import functools
import math

import jax
import jax.numpy as jnp
from jax import lax
from jax.experimental import pallas as pl
from jax.experimental.pallas import tpu as pltpu
from jax.sharding import PartitionSpec as P

MESH = pl.DeviceIdType.MESH
CHUNKS = 2
ALL = (0, 1, 2, 3, 4, 5)
AHEAD = (2, 3, 4, 5)
HELD = (0, 1)
GROUP_Y = 4
GROUP_Z = 4
SLOTS = GROUP_Y * GROUP_Z
NEAR = tuple((a, b) for a in range(2) for b in range(GROUP_Z) if (a, b) != (0, 0))
FULL = tuple((a, b) for a in range(GROUP_Y) for b in range(GROUP_Z) if (a, b) != (0, 0))
BF16 = jnp.bfloat16
F32 = jnp.float32
NT = (((1,), (1,)), ((), ()))


def flipped(gy, a):
    return (gy, gy + 1 - 2 * (gy % 2), (gy + 2) % 4, 3 - gy)[a]


def kernel(
    sizes,
    res_hbm,
    scale_hbm,
    basis_hbm,
    index_hbm,
    inverse_hbm,
    tiles_hbm,
    cols_hbm,
    count_hbm,
    region_smem,
    visc_hbm,
    out_hbm,
    index_smem,
    cols_smem,
    count_smem,
    visc_smem,
    lin,
    scale,
    basis,
    inverse,
    tiles,
    index_all,
    field,
    weighted,
    corr,
    zpack,
    x_low,
    x_high,
    y_low,
    y_high,
    z_low,
    z_high,
    parts,
    part_own,
    picked_rows,
    split_rows,
    gathered,
    load_sem,
    in_sem,
    out_sem,
    face_send,
    face_recv,
    index_send,
    index_recv,
    part_send,
    part_recv,
):
    n_gx, n_gy, n_gz, rhs, blocks, comps, slots = sizes
    rows = rhs // CHUNKS
    gx, gy, gz = lax.axis_index("gx"), lax.axis_index("gy"), lax.axis_index("gz")

    sides = (
        (gx > 0, (gx - 1, gy, gz)),
        (gx < n_gx - 1, (gx + 1, gy, gz)),
        (gy > 0, (gx, gy - 1, gz)),
        (gy < n_gy - 1, (gx, gy + 1, gz)),
        (gz > 0, (gx, gy, gz - 1)),
        (gz < n_gz - 1, (gx, gy, gz + 1)),
    )

    def peer(a, b):
        return (gx, flipped(gy, a), (gz + b) % GROUP_Z)

    def load_chunk(c):
        span = pl.ds(c * rows * blocks, rows * blocks)
        return pltpu.make_async_copy(res_hbm.at[span], lin.at[span], in_sem.at[c])

    loads = (
        pltpu.make_async_copy(index_hbm, index_all.at[0], load_sem.at[0]),
        pltpu.make_async_copy(scale_hbm, scale, load_sem.at[1]),
        pltpu.make_async_copy(inverse_hbm, inverse, load_sem.at[2]),
        pltpu.make_async_copy(basis_hbm, basis, load_sem.at[3]),
        pltpu.make_async_copy(tiles_hbm, tiles, load_sem.at[4]),
        pltpu.make_async_copy(index_hbm, index_smem, load_sem.at[5]),
        pltpu.make_async_copy(cols_hbm, cols_smem, load_sem.at[6]),
        pltpu.make_async_copy(count_hbm, count_smem, load_sem.at[7]),
        pltpu.make_async_copy(visc_hbm, visc_smem, load_sem.at[8]),
    )
    loads[0].start()
    for c in range(CHUNKS):
        load_chunk(c).start()
    for copy in loads[5:]:
        copy.start()
    for copy in loads[1:5]:
        copy.start()

    barrier = pltpu.get_barrier_semaphore()
    expected = 0
    for there, device in sides:

        @pl.when(there)
        def _():
            pl.semaphore_signal(barrier, inc=1, device_id=device, device_id_type=MESH)

        expected = expected + there.astype(jnp.int32)
    for a, b in FULL:
        pl.semaphore_signal(barrier, inc=1, device_id=peer(a, b), device_id_type=MESH)
    pl.semaphore_wait(barrier, expected + len(FULL))

    loads[0].wait()

    def index_copy(a, b):
        k = a * GROUP_Z + b
        return pltpu.make_async_remote_copy(
            src_ref=index_all.at[0],
            dst_ref=index_all.at[k],
            send_sem=index_send.at[k],
            recv_sem=index_recv.at[k],
            device_id=peer(a, b),
            device_id_type=MESH,
        )

    for a, b in FULL:
        index_copy(a, b).start()

    lane = lax.broadcasted_iota(jnp.int32, (rows, 128), 1)

    def face_copies(phase, source, c):
        pairs = (
            (source.at[c, :, 0], x_high),
            (source.at[c, :, 3], x_low),
            (source.at[c, :, :, 0], y_high),
            (source.at[c, :, :, 3], y_low),
            (zpack.at[phase, c], z_high),
            (zpack.at[phase, c], z_low),
        )
        return [
            pltpu.make_async_remote_copy(
                src_ref=src,
                dst_ref=dst.at[phase, c],
                send_sem=face_send.at[phase, c, side],
                recv_sem=face_recv.at[phase, c, side ^ 1],
                device_id=sides[side][1],
                device_id_type=MESH,
            )
            for side, (src, dst) in enumerate(pairs)
        ]

    landing = (x_low, x_high, y_low, y_high, z_low, z_high)

    def send_faces(phase, source, c, chosen=tuple(range(6))):
        for side, copy in enumerate(face_copies(phase, source, c)):
            if side not in chosen:
                continue

            @pl.when(sides[side][0])
            def _():
                copy.start()

    def await_faces(phase, source, c):
        for side, copy in enumerate(face_copies(phase, source, c)):
            land = landing[side].at[phase, c]
            arrived = pltpu.make_async_remote_copy(
                src_ref=land,
                dst_ref=land,
                send_sem=face_send.at[phase, c, side],
                recv_sem=face_recv.at[phase, c, side],
                device_id=sides[side][1],
                device_id_type=MESH,
            )

            @pl.when(sides[side][0])
            def _():
                arrived.wait_recv()

    def drain_faces(phase, source, c):
        for side, copy in enumerate(face_copies(phase, source, c)):

            @pl.when(sides[side][0])
            def _():
                copy.wait_send()

    for side in range(6):

        @pl.when(jnp.logical_not(sides[side][0]))
        def _():
            landing[side][...] = jnp.zeros_like(landing[side])

    def packed(acc, value, b):
        return jnp.where(lane // 2 == b, pltpu.roll(value, 2 * b + 1, 1), acc)

    def pack_first(c):
        def body(comp, acc):
            for x in range(4):
                for y in range(4):
                    b = comp * 16 + x * 4 + y
                    value = lin[pl.ds(c * rows * blocks + b, rows, stride=blocks), :]
                    field[c, comp, x, y] = value
                    acc = packed(acc, value, b)
            return acc

        zpack[0, c] = lax.fori_loop(0, comps, body, jnp.zeros((rows, 128), F32))

    def interface_sum(phase, source, c, emit):
        low = pltpu.roll(z_low[phase, c], 1, 1)
        high = pltpu.roll(z_high[phase, c], 127, 1)
        ends = jnp.where(lane % 2 == 1, low, high)
        edge = (lane == 0) | (lane == 127)

        def body(comp, carry):
            for x in range(4):
                for y in range(4):
                    b = comp * 16 + x * 4 + y
                    total = source[c, comp, x, y]
                    total = total + jnp.where(edge, pltpu.roll(ends, 127 - 2 * b, 1), 0.0)
                    if x == 0:
                        total = total + x_low[phase, c, comp, y]
                    if x == 3:
                        total = total + x_high[phase, c, comp, y]
                    if y == 0:
                        total = total + y_low[phase, c, comp, x]
                    if y == 3:
                        total = total + y_high[phase, c, comp, x]
                    emit(b, total * scale[pl.ds(b, 1), :])
            return carry

        lax.fori_loop(0, comps, body, 0)

    for c in range(CHUNKS):
        load_chunk(c).wait()
        pack_first(c)
        send_faces(0, field, c, AHEAD if c else ALL)

    for copy in loads[5:]:
        copy.wait()

    loads[2].wait()

    def pick_row(p, carry):
        picked_rows[pl.ds(p, 1), :] = inverse[pl.ds(index_smem[0, p], 1), :]
        return carry

    lax.fori_loop(0, 128, pick_row, 0, unroll=8)
    rows_f32 = picked_rows[...]
    high_part = rows_f32.astype(BF16)
    split_rows[0:128, :] = high_part
    split_rows[128:256, :] = (rows_f32 - high_part.astype(F32)).astype(BF16)

    for a, b in FULL:
        index_copy(a, b).wait_recv()

    def pick_columns(k, carry):
        coarse = split_rows.shape[1]
        ids = lax.broadcasted_iota(jnp.int32, (coarse, 128), 0)
        one_hot = jnp.where(ids == index_all[k], 1.0, 0.0).astype(BF16)
        found = jnp.dot(split_rows[...], one_hot, preferred_element_type=F32).astype(BF16)
        gathered[k] = found
        return carry

    lax.fori_loop(0, SLOTS, pick_columns, 0)

    def part_copy(c, a, b, forward):
        slot = (a + 2) * GROUP_Z + b if forward else a * GROUP_Z + b
        return pltpu.make_async_remote_copy(
            src_ref=parts.at[c, 2 * GROUP_Z] if forward else part_own.at[c],
            dst_ref=parts.at[c, slot],
            send_sem=part_send.at[c, slot],
            recv_sem=part_recv.at[c, slot],
            device_id=peer(a, b),
            device_id_type=MESH,
        )

    loads[1].wait()
    loads[3].wait()
    visc = jnp.full((rows, 128), visc_smem[0, region_smem[0, 0, 0]], F32)
    inv_visc = 1.0 / visc
    coarse_scale = math.sqrt(blocks * 128 / 128)

    for c in range(CHUNKS):
        await_faces(0, field, c)

        def keep(b, value):
            weighted[c, b] = value.astype(BF16)

        interface_sum(0, field, c, keep)
        weighted[c, blocks] = jnp.zeros((rows, 128), BF16)

        def restrict(comp, acc):
            lhs = jnp.concatenate([weighted[c, comp * 16 + j] for j in range(16)], axis=1)
            rhs_part = basis[:, pl.ds(pl.multiple_of(comp * 2048, 2048), 2048)]
            return acc + lax.dot_general(lhs, rhs_part, NT, preferred_element_type=F32)

        part = lax.fori_loop(0, comps, restrict, jnp.zeros((rows, 128), F32))
        part_own[c] = part
        parts[c, 0] = part
        part_copy(c, 2, 0, False).start()
        for a, b in NEAR:
            part_copy(c, a, b, False).start()
        if c > 0:
            send_faces(1, corr, c - 1, HELD)
        if c + 1 < CHUNKS:
            send_faces(0, field, c + 1, HELD)
        if c == 0:
            loads[4].wait()

        def schur_row(r, carry):
            picks = [
                weighted[c, jnp.where(k < count_smem[0, r], cols_smem[k, 0, r], blocks)]
                for k in range(slots)
            ]
            lhs = jnp.concatenate(picks, axis=1)
            tile = jnp.concatenate([tiles[r, k] for k in range(slots)], axis=1)
            product = lax.dot_general(lhs, tile, NT, preferred_element_type=F32)
            corr[c, r // 16, (r // 4) % 4, r % 4] = product * inv_visc
            return carry

        lax.fori_loop(0, 12, schur_row, 0, unroll=2)
        part_copy(c, 2, 0, False).wait_recv()
        for a, b in NEAR:
            part_copy(c, a, b, True).start()
        lax.fori_loop(12, blocks, schur_row, 0, unroll=2)
        for a, b in NEAR:
            part_copy(c, a, b, False).wait_recv()
            part_copy(c, a, b, True).wait_recv()

        everyone = jnp.concatenate([parts[c, k] for k in range(SLOTS)], axis=1)
        top = everyone.astype(BF16)
        rest = (everyone - top.astype(F32)).astype(BF16)
        inv_high = jnp.concatenate([gathered[k, 0:128] for k in range(SLOTS)], axis=1)
        inv_low = jnp.concatenate([gathered[k, 128:256] for k in range(SLOTS)], axis=1)
        local = lax.dot_general(top, inv_high, NT, preferred_element_type=F32)
        local = local + lax.dot_general(rest, inv_high, NT, preferred_element_type=F32)
        local = local + lax.dot_general(top, inv_low, NT, preferred_element_type=F32)
        local = local.astype(BF16)

        def prolong(comp, acc):
            rhs_part = basis[:, pl.ds(pl.multiple_of(comp * 2048, 2048), 2048)]
            fix = jnp.dot(local, rhs_part, preferred_element_type=F32) * coarse_scale
            for x in range(4):
                for y in range(4):
                    j = x * 4 + y
                    value = corr[c, comp, x, y] + fix[:, j * 128 : (j + 1) * 128]
                    corr[c, comp, x, y] = value
                    acc = packed(acc, value, comp * 16 + j)
            return acc

        zpack[1, c] = lax.fori_loop(0, comps, prolong, jnp.zeros((rows, 128), F32))
        send_faces(1, corr, c, AHEAD if c + 1 < CHUNKS else ALL)

    def store_chunk(c):
        span = pl.ds(c * rows * blocks, rows * blocks)
        return pltpu.make_async_copy(lin.at[span], out_hbm.at[span], out_sem.at[c])

    for c in range(CHUNKS):
        await_faces(1, corr, c)

        def emit(b, value):
            lin[pl.ds(c * rows * blocks + b, rows, stride=blocks), :] = value

        interface_sum(1, corr, c, emit)
        store_chunk(c).start()

    for c in range(CHUNKS):
        drain_faces(0, field, c)
        drain_faces(1, corr, c)
        part_copy(c, 2, 0, False).wait_send()
        for a, b in NEAR:
            part_copy(c, a, b, False).wait_send()
            part_copy(c, a, b, True).wait_send()
        store_chunk(c).wait()
    for a, b in FULL:
        index_copy(a, b).wait_send()


def per_device(
    residual,
    interface_scaling,
    primal_basis,
    primal_index,
    coarse_inverse,
    schur_tiles,
    tile_cols,
    tile_count,
    region_id,
    region_viscosity,
):
    rhs, comps, cells_x, cells_y, cells_z = residual.shape
    blocks = comps * cells_x * cells_y
    slots = schur_tiles.shape[4]
    primal = primal_basis.shape[3]
    coarse = coarse_inverse.shape[1]
    rows = rhs // CHUNKS
    sizes = (
        lax.axis_size("gx"),
        lax.axis_size("gy"),
        lax.axis_size("gz"),
        rhs,
        blocks,
        comps,
        slots,
    )
    face = pltpu.VMEM((2, CHUNKS, comps, cells_x, rows, cells_z), F32)
    ends = pltpu.VMEM((2, CHUNKS, rows, cells_z), F32)
    dma = pltpu.SemaphoreType.DMA
    hbm = pl.BlockSpec(memory_space=pltpu.HBM)
    out = pl.pallas_call(
        functools.partial(kernel, sizes),
        out_shape=jax.ShapeDtypeStruct((rhs * blocks, cells_z), F32),
        in_specs=[hbm] * 8 + [pl.BlockSpec(memory_space=pltpu.SMEM), hbm],
        out_specs=hbm,
        scratch_shapes=[
            pltpu.SMEM((1, primal), jnp.int32),
            pltpu.SMEM((slots, 1, blocks), jnp.int32),
            pltpu.SMEM((1, blocks), jnp.int32),
            pltpu.SMEM((1, region_viscosity.shape[0]), F32),
            pltpu.VMEM((rhs * blocks, cells_z), F32),
            pltpu.VMEM((blocks, cells_z), F32),
            pltpu.VMEM((primal, blocks * cells_z), BF16),
            pltpu.VMEM((coarse, coarse), F32),
            pltpu.VMEM((blocks, slots, cells_z, cells_z), BF16),
            pltpu.VMEM((SLOTS, 1, primal), jnp.int32),
            pltpu.VMEM((CHUNKS, comps, cells_x, cells_y, rows, cells_z), F32),
            pltpu.VMEM((CHUNKS, blocks + 1, rows, cells_z), BF16),
            pltpu.VMEM((CHUNKS, comps, cells_x, cells_y, rows, cells_z), F32),
            ends,
            face,
            face,
            face,
            face,
            ends,
            ends,
            pltpu.VMEM((CHUNKS, SLOTS, rows, primal), F32),
            pltpu.VMEM((CHUNKS, rows, primal), F32),
            pltpu.VMEM((primal, coarse), F32),
            pltpu.VMEM((2 * primal, coarse), BF16),
            pltpu.VMEM((SLOTS, 2 * primal, primal), BF16),
            dma((9,)),
            dma((CHUNKS,)),
            dma((CHUNKS,)),
            dma((2, CHUNKS, 6)),
            dma((2, CHUNKS, 6)),
            dma((SLOTS,)),
            dma((SLOTS,)),
            dma((CHUNKS, SLOTS)),
            dma((CHUNKS, SLOTS)),
        ],
        compiler_params=pltpu.CompilerParams(
            collective_id=0, has_side_effects=True, vmem_limit_bytes=60 * 2**20
        ),
    )(
        residual.reshape(rhs * blocks, cells_z),
        interface_scaling.reshape(blocks, cells_z),
        primal_basis.reshape(primal, blocks * cells_z),
        primal_index.reshape(1, primal),
        coarse_inverse,
        schur_tiles.reshape(blocks, slots, cells_z, cells_z),
        tile_cols.transpose(0, 1, 4, 2, 3).reshape(slots, 1, blocks),
        tile_count.reshape(1, blocks),
        region_id,
        region_viscosity.reshape(1, -1),
    )
    return out.reshape(residual.shape)


def solution(mesh):
    in_specs = (
        P(None, None, "gx", "gy", "gz"),
        P(None, "gx", "gy", "gz"),
        P("gx", "gy", "gz", None, None),
        P("gx", "gy", "gz", None),
        P("gx", None),
        P("gx", "gy", "gz", None, None, None, None),
        P("gx", "gy", "gz", None, None),
        P("gx", "gy", "gz", None),
        P("gx", "gy", "gz"),
        P(),
    )
    out_specs = P(None, None, "gx", "gy", "gz")
    return jax.shard_map(
        per_device, mesh=mesh, in_specs=in_specs, out_specs=out_specs, check_vma=False
    )
```

```python
import functools
import math

import jax
import jax.numpy as jnp
from jax import lax
from jax.experimental import pallas as pl
from jax.experimental.pallas import tpu as pltpu
from jax.sharding import PartitionSpec as P

MESH = pl.DeviceIdType.MESH
CHUNKS = 2
ALL = (0, 1, 2, 3, 4, 5)
AHEAD = (2, 3, 4, 5)
HELD = (0, 1)
GROUP_Y = 4
GROUP_Z = 4
SLOTS = GROUP_Y * GROUP_Z
NEAR = tuple((a, b) for a in range(2) for b in range(GROUP_Z) if (a, b) != (0, 0))
FULL = tuple((a, b) for a in range(GROUP_Y) for b in range(GROUP_Z) if (a, b) != (0, 0))
BF16 = jnp.bfloat16
F32 = jnp.float32
NT = (((1,), (1,)), ((), ()))


def flipped(gy, a):
    return (gy, gy + 1 - 2 * (gy % 2), (gy + 2) % 4, 3 - gy)[a]


def kernel(
    sizes,
    res_hbm,
    scale_hbm,
    basis_hbm,
    index_hbm,
    inverse_hbm,
    tiles_hbm,
    cols_hbm,
    count_hbm,
    region_smem,
    visc_hbm,
    out_hbm,
    index_smem,
    cols_smem,
    count_smem,
    visc_smem,
    lin,
    scale,
    basis,
    inverse,
    tiles,
    index_all,
    field,
    weighted,
    corr,
    zpack,
    x_low,
    x_high,
    y_low,
    y_high,
    z_low,
    z_high,
    parts,
    part_own,
    picked_rows,
    split_rows,
    gathered,
    load_sem,
    in_sem,
    out_sem,
    face_send,
    face_recv,
    index_send,
    index_recv,
    part_send,
    part_recv,
):
    n_gx, n_gy, n_gz, rhs, blocks, comps, slots = sizes
    rows = rhs // CHUNKS
    gx, gy, gz = lax.axis_index("gx"), lax.axis_index("gy"), lax.axis_index("gz")

    sides = (
        (gx > 0, (gx - 1, gy, gz)),
        (gx < n_gx - 1, (gx + 1, gy, gz)),
        (gy > 0, (gx, gy - 1, gz)),
        (gy < n_gy - 1, (gx, gy + 1, gz)),
        (gz > 0, (gx, gy, gz - 1)),
        (gz < n_gz - 1, (gx, gy, gz + 1)),
    )

    def peer(a, b):
        return (gx, flipped(gy, a), (gz + b) % GROUP_Z)

    def load_chunk(c):
        span = pl.ds(c * rows * blocks, rows * blocks)
        return pltpu.make_async_copy(res_hbm.at[span], lin.at[span], in_sem.at[c])

    loads = (
        pltpu.make_async_copy(index_hbm, index_all.at[0], load_sem.at[0]),
        pltpu.make_async_copy(scale_hbm, scale, load_sem.at[1]),
        pltpu.make_async_copy(inverse_hbm, inverse, load_sem.at[2]),
        pltpu.make_async_copy(basis_hbm, basis, load_sem.at[3]),
        pltpu.make_async_copy(tiles_hbm, tiles, load_sem.at[4]),
        pltpu.make_async_copy(index_hbm, index_smem, load_sem.at[5]),
        pltpu.make_async_copy(cols_hbm, cols_smem, load_sem.at[6]),
        pltpu.make_async_copy(count_hbm, count_smem, load_sem.at[7]),
        pltpu.make_async_copy(visc_hbm, visc_smem, load_sem.at[8]),
    )
    for c in range(CHUNKS):
        load_chunk(c).start()
    loads[0].start()
    for copy in loads[5:]:
        copy.start()

    barrier = pltpu.get_barrier_semaphore()
    expected = 0
    for there, device in sides:

        @pl.when(there)
        def _():
            pl.semaphore_signal(barrier, inc=1, device_id=device, device_id_type=MESH)

        expected = expected + there.astype(jnp.int32)
    for a, b in FULL:
        pl.semaphore_signal(barrier, inc=1, device_id=peer(a, b), device_id_type=MESH)

    def index_copy(a, b):
        k = a * GROUP_Z + b
        return pltpu.make_async_remote_copy(
            src_ref=index_all.at[0],
            dst_ref=index_all.at[k],
            send_sem=index_send.at[k],
            recv_sem=index_recv.at[k],
            device_id=peer(a, b),
            device_id_type=MESH,
        )

    lane = lax.broadcasted_iota(jnp.int32, (rows, 128), 1)

    def face_copies(phase, source, c):
        pairs = (
            (source.at[c, :, 0], x_high),
            (source.at[c, :, 3], x_low),
            (source.at[c, :, :, 0], y_high),
            (source.at[c, :, :, 3], y_low),
            (zpack.at[phase, c], z_high),
            (zpack.at[phase, c], z_low),
        )
        return [
            pltpu.make_async_remote_copy(
                src_ref=src,
                dst_ref=dst.at[phase, c],
                send_sem=face_send.at[phase, c, side],
                recv_sem=face_recv.at[phase, c, side ^ 1],
                device_id=sides[side][1],
                device_id_type=MESH,
            )
            for side, (src, dst) in enumerate(pairs)
        ]

    landing = (x_low, x_high, y_low, y_high, z_low, z_high)

    def send_faces(phase, source, c, chosen=tuple(range(6))):
        for side, copy in enumerate(face_copies(phase, source, c)):
            if side not in chosen:
                continue

            @pl.when(sides[side][0])
            def _():
                copy.start()

    def await_faces(phase, source, c):
        for side, copy in enumerate(face_copies(phase, source, c)):
            land = landing[side].at[phase, c]
            arrived = pltpu.make_async_remote_copy(
                src_ref=land,
                dst_ref=land,
                send_sem=face_send.at[phase, c, side],
                recv_sem=face_recv.at[phase, c, side],
                device_id=sides[side][1],
                device_id_type=MESH,
            )

            @pl.when(sides[side][0])
            def _():
                arrived.wait_recv()

    def drain_faces(phase, source, c):
        for side, copy in enumerate(face_copies(phase, source, c)):

            @pl.when(sides[side][0])
            def _():
                copy.wait_send()

    def packed(acc, value, b):
        return jnp.where(lane // 2 == b, pltpu.roll(value, 2 * b + 1, 1), acc)

    def pack_first(c):
        def body(comp, acc):
            for x in range(4):
                for y in range(4):
                    b = comp * 16 + x * 4 + y
                    value = lin[pl.ds(c * rows * blocks + b, rows, stride=blocks), :]
                    field[c, comp, x, y] = value
                    acc = packed(acc, value, b)
            return acc

        zpack[0, c] = lax.fori_loop(0, comps, body, jnp.zeros((rows, 128), F32))

    def interface_sum(phase, source, c, emit):
        low = pltpu.roll(z_low[phase, c], 1, 1)
        high = pltpu.roll(z_high[phase, c], 127, 1)
        ends = jnp.where(lane % 2 == 1, low, high)
        edge = (lane == 0) | (lane == 127)

        def body(comp, carry):
            for x in range(4):
                for y in range(4):
                    b = comp * 16 + x * 4 + y
                    total = source[c, comp, x, y]
                    total = total + jnp.where(edge, pltpu.roll(ends, 127 - 2 * b, 1), 0.0)
                    if x == 0:
                        total = total + x_low[phase, c, comp, y]
                    if x == 3:
                        total = total + x_high[phase, c, comp, y]
                    if y == 0:
                        total = total + y_low[phase, c, comp, x]
                    if y == 3:
                        total = total + y_high[phase, c, comp, x]
                    emit(b, total * scale[pl.ds(b, 1), :])
            return carry

        lax.fori_loop(0, comps, body, 0)

    load_chunk(0).wait()
    pack_first(0)
    loads[2].start()
    loads[0].wait()
    pl.semaphore_wait(barrier, expected + len(FULL))
    for a, b in FULL:
        index_copy(a, b).start()
    send_faces(0, field, 0)
    for c in range(1, CHUNKS):
        load_chunk(c).wait()
        pack_first(c)
        send_faces(0, field, c, AHEAD)

    for k in (1, 3, 4):
        loads[k].start()

    for side in range(6):

        @pl.when(jnp.logical_not(sides[side][0]))
        def _():
            landing[side][...] = jnp.zeros_like(landing[side])


    for copy in loads[5:]:
        copy.wait()

    loads[2].wait()

    def pick_row(p, carry):
        picked_rows[pl.ds(p, 1), :] = inverse[pl.ds(index_smem[0, p], 1), :]
        return carry

    lax.fori_loop(0, 128, pick_row, 0, unroll=8)
    rows_f32 = picked_rows[...]
    high_part = rows_f32.astype(BF16)
    split_rows[0:128, :] = high_part
    split_rows[128:256, :] = (rows_f32 - high_part.astype(F32)).astype(BF16)

    for a, b in FULL:
        index_copy(a, b).wait_recv()

    def pick_columns(k, carry):
        coarse = split_rows.shape[1]
        ids = lax.broadcasted_iota(jnp.int32, (coarse, 128), 0)
        one_hot = jnp.where(ids == index_all[k], 1.0, 0.0).astype(BF16)
        found = jnp.dot(split_rows[...], one_hot, preferred_element_type=F32).astype(BF16)
        gathered[k] = found
        return carry

    lax.fori_loop(0, SLOTS, pick_columns, 0)

    def part_copy(c, a, b, forward):
        slot = (a + 2) * GROUP_Z + b if forward else a * GROUP_Z + b
        return pltpu.make_async_remote_copy(
            src_ref=parts.at[c, 2 * GROUP_Z] if forward else part_own.at[c],
            dst_ref=parts.at[c, slot],
            send_sem=part_send.at[c, slot],
            recv_sem=part_recv.at[c, slot],
            device_id=peer(a, b),
            device_id_type=MESH,
        )

    loads[1].wait()
    loads[3].wait()
    visc = jnp.full((rows, 128), visc_smem[0, region_smem[0, 0, 0]], F32)
    inv_visc = 1.0 / visc
    coarse_scale = math.sqrt(blocks * 128 / 128)

    for c in range(CHUNKS):
        await_faces(0, field, c)

        def keep(b, value):
            weighted[c, b] = value.astype(BF16)

        interface_sum(0, field, c, keep)
        weighted[c, blocks] = jnp.zeros((rows, 128), BF16)

        def restrict(comp, acc):
            lhs = jnp.concatenate([weighted[c, comp * 16 + j] for j in range(16)], axis=1)
            rhs_part = basis[:, pl.ds(pl.multiple_of(comp * 2048, 2048), 2048)]
            return acc + lax.dot_general(lhs, rhs_part, NT, preferred_element_type=F32)

        part = lax.fori_loop(0, comps, restrict, jnp.zeros((rows, 128), F32))
        part_own[c] = part
        parts[c, 0] = part
        part_copy(c, 2, 0, False).start()
        for a, b in NEAR:
            part_copy(c, a, b, False).start()
        if c > 0:
            send_faces(1, corr, c - 1, HELD)
        if c + 1 < CHUNKS:
            send_faces(0, field, c + 1, HELD)
        if c == 0:
            loads[4].wait()

        def schur_row(r, carry):
            picks = [
                weighted[c, jnp.where(k < count_smem[0, r], cols_smem[k, 0, r], blocks)]
                for k in range(slots)
            ]
            lhs = jnp.concatenate(picks, axis=1)
            tile = jnp.concatenate([tiles[r, k] for k in range(slots)], axis=1)
            product = lax.dot_general(lhs, tile, NT, preferred_element_type=F32)
            corr[c, r // 16, (r // 4) % 4, r % 4] = product * inv_visc
            return carry

        lax.fori_loop(0, 12, schur_row, 0, unroll=2)
        part_copy(c, 2, 0, False).wait_recv()
        for a, b in NEAR:
            part_copy(c, a, b, True).start()
        lax.fori_loop(12, blocks, schur_row, 0, unroll=2)
        for a, b in NEAR:
            part_copy(c, a, b, False).wait_recv()
            part_copy(c, a, b, True).wait_recv()

        everyone = jnp.concatenate([parts[c, k] for k in range(SLOTS)], axis=1)
        top = everyone.astype(BF16)
        rest = (everyone - top.astype(F32)).astype(BF16)
        inv_high = jnp.concatenate([gathered[k, 0:128] for k in range(SLOTS)], axis=1)
        inv_low = jnp.concatenate([gathered[k, 128:256] for k in range(SLOTS)], axis=1)
        local = lax.dot_general(top, inv_high, NT, preferred_element_type=F32)
        local = local + lax.dot_general(rest, inv_high, NT, preferred_element_type=F32)
        local = local + lax.dot_general(top, inv_low, NT, preferred_element_type=F32)
        local = local.astype(BF16)

        def prolong(comp, acc):
            rhs_part = basis[:, pl.ds(pl.multiple_of(comp * 2048, 2048), 2048)]
            fix = jnp.dot(local, rhs_part, preferred_element_type=F32) * coarse_scale
            for x in range(4):
                for y in range(4):
                    j = x * 4 + y
                    value = corr[c, comp, x, y] + fix[:, j * 128 : (j + 1) * 128]
                    corr[c, comp, x, y] = value
                    acc = packed(acc, value, comp * 16 + j)
            return acc

        zpack[1, c] = lax.fori_loop(0, comps, prolong, jnp.zeros((rows, 128), F32))
        send_faces(1, corr, c, AHEAD if c + 1 < CHUNKS else ALL)

    def store_chunk(c):
        span = pl.ds(c * rows * blocks, rows * blocks)
        return pltpu.make_async_copy(lin.at[span], out_hbm.at[span], out_sem.at[c])

    for c in range(CHUNKS):
        await_faces(1, corr, c)

        def emit(b, value):
            lin[pl.ds(c * rows * blocks + b, rows, stride=blocks), :] = value

        interface_sum(1, corr, c, emit)
        store_chunk(c).start()

    for c in range(CHUNKS):
        drain_faces(0, field, c)
        drain_faces(1, corr, c)
        part_copy(c, 2, 0, False).wait_send()
        for a, b in NEAR:
            part_copy(c, a, b, False).wait_send()
            part_copy(c, a, b, True).wait_send()
        store_chunk(c).wait()
    for a, b in FULL:
        index_copy(a, b).wait_send()


def per_device(
    residual,
    interface_scaling,
    primal_basis,
    primal_index,
    coarse_inverse,
    schur_tiles,
    tile_cols,
    tile_count,
    region_id,
    region_viscosity,
):
    rhs, comps, cells_x, cells_y, cells_z = residual.shape
    blocks = comps * cells_x * cells_y
    slots = schur_tiles.shape[4]
    primal = primal_basis.shape[3]
    coarse = coarse_inverse.shape[1]
    rows = rhs // CHUNKS
    sizes = (
        lax.axis_size("gx"),
        lax.axis_size("gy"),
        lax.axis_size("gz"),
        rhs,
        blocks,
        comps,
        slots,
    )
    face = pltpu.VMEM((2, CHUNKS, comps, cells_x, rows, cells_z), F32)
    ends = pltpu.VMEM((2, CHUNKS, rows, cells_z), F32)
    dma = pltpu.SemaphoreType.DMA
    hbm = pl.BlockSpec(memory_space=pltpu.HBM)
    operands = (
        residual.reshape(rhs * blocks, cells_z),
        interface_scaling.reshape(blocks, cells_z),
        primal_basis.reshape(primal, blocks * cells_z),
        primal_index.reshape(1, primal),
        coarse_inverse,
        schur_tiles.reshape(blocks, slots, cells_z, cells_z),
        tile_cols.transpose(0, 1, 4, 2, 3).reshape(slots, 1, blocks),
        tile_count.reshape(1, blocks),
        region_id,
        region_viscosity.reshape(1, -1),
    )
    operands = [
        v if v.size == 1 else pltpu.with_memory_space_constraint(v, pltpu.HBM) for v in operands
    ]
    out = pl.pallas_call(
        functools.partial(kernel, sizes),
        out_shape=jax.ShapeDtypeStruct((rhs * blocks, cells_z), F32),
        in_specs=[hbm] * 8 + [pl.BlockSpec(memory_space=pltpu.SMEM), hbm],
        out_specs=hbm,
        scratch_shapes=[
            pltpu.SMEM((1, primal), jnp.int32),
            pltpu.SMEM((slots, 1, blocks), jnp.int32),
            pltpu.SMEM((1, blocks), jnp.int32),
            pltpu.SMEM((1, region_viscosity.shape[0]), F32),
            pltpu.VMEM((rhs * blocks, cells_z), F32),
            pltpu.VMEM((blocks, cells_z), F32),
            pltpu.VMEM((primal, blocks * cells_z), BF16),
            pltpu.VMEM((coarse, coarse), F32),
            pltpu.VMEM((blocks, slots, cells_z, cells_z), BF16),
            pltpu.VMEM((SLOTS, 1, primal), jnp.int32),
            pltpu.VMEM((CHUNKS, comps, cells_x, cells_y, rows, cells_z), F32),
            pltpu.VMEM((CHUNKS, blocks + 1, rows, cells_z), BF16),
            pltpu.VMEM((CHUNKS, comps, cells_x, cells_y, rows, cells_z), F32),
            ends,
            face,
            face,
            face,
            face,
            ends,
            ends,
            pltpu.VMEM((CHUNKS, SLOTS, rows, primal), F32),
            pltpu.VMEM((CHUNKS, rows, primal), F32),
            pltpu.VMEM((primal, coarse), F32),
            pltpu.VMEM((2 * primal, coarse), BF16),
            pltpu.VMEM((SLOTS, 2 * primal, primal), BF16),
            dma((9,)),
            dma((CHUNKS,)),
            dma((CHUNKS,)),
            dma((2, CHUNKS, 6)),
            dma((2, CHUNKS, 6)),
            dma((SLOTS,)),
            dma((SLOTS,)),
            dma((CHUNKS, SLOTS)),
            dma((CHUNKS, SLOTS)),
        ],
        compiler_params=pltpu.CompilerParams(
            collective_id=0, has_side_effects=True, vmem_limit_bytes=52 * 2**20
        ),
    )(*operands)
    return out.reshape(residual.shape)


def solution(mesh):
    in_specs = (
        P(None, None, "gx", "gy", "gz"),
        P(None, "gx", "gy", "gz"),
        P("gx", "gy", "gz", None, None),
        P("gx", "gy", "gz", None),
        P("gx", None),
        P("gx", "gy", "gz", None, None, None, None),
        P("gx", "gy", "gz", None, None),
        P("gx", "gy", "gz", None),
        P("gx", "gy", "gz"),
        P(),
    )
    out_specs = P(None, None, "gx", "gy", "gz")
    return jax.shard_map(
        per_device, mesh=mesh, in_specs=in_specs, out_specs=out_specs, check_vma=False
    )
```

```python
import functools
import math

import jax
import jax.numpy as jnp
from jax import lax
from jax.experimental import pallas as pl
from jax.experimental.pallas import tpu as pltpu
from jax.sharding import PartitionSpec as P

MESH = pl.DeviceIdType.MESH
CHUNKS = 2
AHEAD = 0
INNER = (1, 2)
OUTER = (0, 3)
GROUP_Y = 4
GROUP_Z = 4
SLOTS = GROUP_Y * GROUP_Z
NEAR = tuple((a, b) for a in range(2) for b in range(GROUP_Z) if (a, b) != (0, 0))
FULL = tuple((a, b) for a in range(GROUP_Y) for b in range(GROUP_Z) if (a, b) != (0, 0))
BF16 = jnp.bfloat16
F32 = jnp.float32
NT = (((1,), (1,)), ((), ()))


def flipped(gy, a):
    return (gy, gy + 1 - 2 * (gy % 2), (gy + 2) % 4, 3 - gy)[a]


def kernel(
    sizes,
    res_hbm,
    scale_hbm,
    basis_hbm,
    index_hbm,
    inverse_hbm,
    tiles_hbm,
    cols_hbm,
    count_hbm,
    region_smem,
    visc_hbm,
    out,
    index_smem,
    cols_smem,
    count_smem,
    visc_smem,
    lin,
    scale,
    basis,
    inverse,
    tiles,
    index_all,
    field,
    weighted,
    corr,
    zpack,
    x_low,
    x_high,
    y_low,
    y_high,
    z_low,
    z_high,
    parts,
    part_own,
    picked_rows,
    split_rows,
    gathered,
    load_sem,
    in_sem,
    face_send,
    face_recv,
    index_send,
    index_recv,
    part_send,
    part_recv,
):
    n_gx, n_gy, n_gz, rhs, blocks, comps, slots = sizes
    rows = rhs // CHUNKS
    gx, gy, gz = lax.axis_index("gx"), lax.axis_index("gy"), lax.axis_index("gz")

    sides = (
        (gx > 0, (gx - 1, gy, gz)),
        (gx < n_gx - 1, (gx + 1, gy, gz)),
        (gy > 0, (gx, gy - 1, gz)),
        (gy < n_gy - 1, (gx, gy + 1, gz)),
        (gz > 0, (gx, gy, gz - 1)),
        (gz < n_gz - 1, (gx, gy, gz + 1)),
    )

    def peer(a, b):
        return (gx, flipped(gy, a), (gz + b) % GROUP_Z)

    def load_chunk(c):
        span = pl.ds(c * rows * blocks, rows * blocks)
        return pltpu.make_async_copy(res_hbm.at[span], lin.at[span], in_sem.at[c])

    loads = (
        pltpu.make_async_copy(index_hbm, index_all.at[0], load_sem.at[0]),
        pltpu.make_async_copy(scale_hbm, scale, load_sem.at[1]),
        pltpu.make_async_copy(inverse_hbm, inverse, load_sem.at[2]),
        pltpu.make_async_copy(basis_hbm, basis, load_sem.at[3]),
        pltpu.make_async_copy(tiles_hbm, tiles, load_sem.at[4]),
        pltpu.make_async_copy(index_hbm, index_smem, load_sem.at[5]),
        pltpu.make_async_copy(cols_hbm, cols_smem, load_sem.at[6]),
        pltpu.make_async_copy(count_hbm, count_smem, load_sem.at[7]),
        pltpu.make_async_copy(visc_hbm, visc_smem, load_sem.at[8]),
    )
    for c in range(CHUNKS):
        load_chunk(c).start()
    loads[0].start()
    for copy in loads[5:]:
        copy.start()

    barrier = pltpu.get_barrier_semaphore()
    expected = 0
    for there, device in sides:

        @pl.when(there)
        def _():
            pl.semaphore_signal(barrier, inc=1, device_id=device, device_id_type=MESH)

        expected = expected + there.astype(jnp.int32)
    for a, b in FULL:
        pl.semaphore_signal(barrier, inc=1, device_id=peer(a, b), device_id_type=MESH)

    def index_copy(a, b):
        k = a * GROUP_Z + b
        return pltpu.make_async_remote_copy(
            src_ref=index_all.at[0],
            dst_ref=index_all.at[k],
            send_sem=index_send.at[k],
            recv_sem=index_recv.at[k],
            device_id=peer(a, b),
            device_id_type=MESH,
        )

    lane = lax.broadcasted_iota(jnp.int32, (rows, 128), 1)

    def face_copies(phase, source, c):
        pairs = (
            (source.at[c, :, 0], x_high),
            (source.at[c, :, 3], x_low),
            (source.at[c, :, :, 0], y_high),
            (source.at[c, :, :, 3], y_low),
            (zpack.at[phase, c], z_high),
            (zpack.at[phase, c], z_low),
        )
        return [
            pltpu.make_async_remote_copy(
                src_ref=src,
                dst_ref=dst.at[phase, c],
                send_sem=face_send.at[phase, c, side],
                recv_sem=face_recv.at[phase, c, side ^ 1],
                device_id=sides[side][1],
                device_id_type=MESH,
            )
            for side, (src, dst) in enumerate(pairs)
        ]

    landing = (x_low, x_high, y_low, y_high, z_low, z_high)

    def x_copy(phase, source, c, side, comp):
        return pltpu.make_async_remote_copy(
            src_ref=source.at[c, comp, 3 * side],
            dst_ref=(x_high, x_low)[side].at[phase, c, comp],
            send_sem=face_send.at[phase, c, side],
            recv_sem=face_recv.at[phase, c, 1 - side],
            device_id=sides[side][1],
            device_id_type=MESH,
        )

    def send_faces(phase, source, c):
        for side in (4, 5, 2, 3):

            @pl.when(sides[side][0])
            def _():
                face_copies(phase, source, c)[side].start()

    def send_x(phase, source, c, first, last):
        for comp in range(first, last):
            for side in range(2):

                @pl.when(sides[side][0])
                def _():
                    x_copy(phase, source, c, side, comp).start()

    def await_faces(phase, c, chosen):
        for side in chosen:
            land = landing[side].at[phase, c]
            arrived = pltpu.make_async_remote_copy(
                src_ref=land,
                dst_ref=land,
                send_sem=face_send.at[phase, c, side],
                recv_sem=face_recv.at[phase, c, side],
                device_id=sides[side][1],
                device_id_type=MESH,
            )

            @pl.when(sides[side][0])
            def _():
                arrived.wait_recv()

    def drain_faces(phase, source, c):
        for side, copy in enumerate(face_copies(phase, source, c)):

            @pl.when(sides[side][0])
            def _():
                copy.wait_send()

    def packed(acc, value, b):
        return jnp.where(lane // 2 == b, pltpu.roll(value, 2 * b + 1, 1), acc)

    def pack_first(c):
        def body(comp, acc):
            for x in range(4):
                for y in range(4):
                    b = comp * 16 + x * 4 + y
                    value = lin[pl.ds(c * rows * blocks + b, rows, stride=blocks), :]
                    field[c, comp, x, y] = value
                    acc = packed(acc, value, b)
            return acc

        zpack[0, c] = lax.fori_loop(0, comps, body, jnp.zeros((rows, 128), F32))

    def interface_sum(phase, source, c, planes, emit):
        low = pltpu.roll(z_low[phase, c], 1, 1)
        high = pltpu.roll(z_high[phase, c], 127, 1)
        ends = jnp.where(lane % 2 == 1, low, high)
        edge = (lane == 0) | (lane == 127)

        def body(comp, carry):
            for x in planes:
                for y in range(4):
                    b = comp * 16 + x * 4 + y
                    total = source[c, comp, x, y]
                    total = total + jnp.where(edge, pltpu.roll(ends, 127 - 2 * b, 1), 0.0)
                    if x == 0:
                        total = total + x_low[phase, c, comp, y]
                    if x == 3:
                        total = total + x_high[phase, c, comp, y]
                    if y == 0:
                        total = total + y_low[phase, c, comp, x]
                    if y == 3:
                        total = total + y_high[phase, c, comp, x]
                    emit(b, total * scale[pl.ds(b, 1), :])
            return carry

        lax.fori_loop(0, comps, body, 0)

    load_chunk(0).wait()
    pack_first(0)
    loads[2].start()
    loads[0].wait()
    pl.semaphore_wait(barrier, expected + len(FULL))
    for a, b in FULL:
        index_copy(a, b).start()
    send_faces(0, field, 0)
    send_x(0, field, 0, 0, comps)
    for c in range(1, CHUNKS):
        load_chunk(c).wait()
        pack_first(c)
        send_faces(0, field, c)
        send_x(0, field, c, 0, AHEAD)

    for k in (1, 3, 4):
        loads[k].start()

    for side in range(6):

        @pl.when(jnp.logical_not(sides[side][0]))
        def _():
            landing[side][...] = jnp.zeros_like(landing[side])


    for copy in loads[5:]:
        copy.wait()

    loads[2].wait()

    def pick_row(p, carry):
        picked_rows[pl.ds(p, 1), :] = inverse[pl.ds(index_smem[0, p], 1), :]
        return carry

    lax.fori_loop(0, 128, pick_row, 0, unroll=8)
    rows_f32 = picked_rows[...]
    high_part = rows_f32.astype(BF16)
    split_rows[0:128, :] = high_part
    split_rows[128:256, :] = (rows_f32 - high_part.astype(F32)).astype(BF16)

    for a, b in FULL:
        index_copy(a, b).wait_recv()

    def pick_columns(k, carry):
        coarse = split_rows.shape[1]
        ids = lax.broadcasted_iota(jnp.int32, (coarse, 128), 0)
        one_hot = jnp.where(ids == index_all[k], 1.0, 0.0).astype(BF16)
        found = jnp.dot(split_rows[...], one_hot, preferred_element_type=F32).astype(BF16)
        gathered[k] = found
        return carry

    lax.fori_loop(0, SLOTS, pick_columns, 0)

    def part_copy(c, a, b, forward):
        slot = (a + 2) * GROUP_Z + b if forward else a * GROUP_Z + b
        return pltpu.make_async_remote_copy(
            src_ref=parts.at[c, 2 * GROUP_Z] if forward else part_own.at[c],
            dst_ref=parts.at[c, slot],
            send_sem=part_send.at[c, slot],
            recv_sem=part_recv.at[c, slot],
            device_id=peer(a, b),
            device_id_type=MESH,
        )

    loads[1].wait()
    loads[3].wait()
    visc = jnp.full((rows, 128), visc_smem[0, region_smem[0, 0, 0]], F32)
    inv_visc = 1.0 / visc
    coarse_scale = math.sqrt(blocks * 128 / 128)

    for c in range(CHUNKS):
        def keep(b, value):
            weighted[c, b] = value.astype(BF16)

        def restrict(planes):
            def body(comp, acc):
                picks = [weighted[c, comp * 16 + x * 4 + y] for x in planes for y in range(4)]
                spans = [
                    basis[:, pl.ds(pl.multiple_of(comp * 2048 + x * 512, 512), 512)] for x in planes
                ]
                return acc + lax.dot_general(
                    jnp.concatenate(picks, axis=1),
                    jnp.concatenate(spans, axis=1),
                    NT,
                    preferred_element_type=F32,
                )

            return body

        await_faces(0, c, (2, 3, 4, 5))
        interface_sum(0, field, c, INNER, keep)
        part = lax.fori_loop(0, comps, restrict(INNER), jnp.zeros((rows, 128), F32))
        await_faces(0, c, (0, 1))
        interface_sum(0, field, c, OUTER, keep)
        weighted[c, blocks] = jnp.zeros((rows, 128), BF16)
        part = lax.fori_loop(0, comps, restrict(OUTER), part)
        part_own[c] = part
        parts[c, 0] = part
        part_copy(c, 2, 0, False).start()
        for a, b in NEAR:
            part_copy(c, a, b, False).start()
        if c > 0:
            send_x(1, corr, c - 1, AHEAD, comps)
        if c + 1 < CHUNKS:
            send_x(0, field, c + 1, AHEAD, comps)
        if c == 0:
            loads[4].wait()

        def schur_row(r, carry):
            picks = [
                weighted[c, jnp.where(k < count_smem[0, r], cols_smem[k, 0, r], blocks)]
                for k in range(slots)
            ]
            lhs = jnp.concatenate(picks, axis=1)
            tile = jnp.concatenate([tiles[r, k] for k in range(slots)], axis=1)
            product = lax.dot_general(lhs, tile, NT, preferred_element_type=F32)
            corr[c, r // 16, (r // 4) % 4, r % 4] = product * inv_visc
            return carry

        lax.fori_loop(0, 12, schur_row, 0, unroll=2)
        part_copy(c, 2, 0, False).wait_recv()
        for a, b in NEAR:
            part_copy(c, a, b, True).start()
        lax.fori_loop(12, blocks, schur_row, 0, unroll=2)
        for a, b in NEAR:
            part_copy(c, a, b, False).wait_recv()
            part_copy(c, a, b, True).wait_recv()

        everyone = jnp.concatenate([parts[c, k] for k in range(SLOTS)], axis=1)
        top = everyone.astype(BF16)
        rest = (everyone - top.astype(F32)).astype(BF16)
        inv_high = jnp.concatenate([gathered[k, 0:128] for k in range(SLOTS)], axis=1)
        inv_low = jnp.concatenate([gathered[k, 128:256] for k in range(SLOTS)], axis=1)
        local = lax.dot_general(top, inv_high, NT, preferred_element_type=F32)
        local = local + lax.dot_general(rest, inv_high, NT, preferred_element_type=F32)
        local = local + lax.dot_general(top, inv_low, NT, preferred_element_type=F32)
        local = local.astype(BF16)

        def prolong(comp, acc):
            rhs_part = basis[:, pl.ds(pl.multiple_of(comp * 2048, 2048), 2048)]
            fix = jnp.dot(local, rhs_part, preferred_element_type=F32) * coarse_scale
            for x in range(4):
                for y in range(4):
                    j = x * 4 + y
                    value = corr[c, comp, x, y] + fix[:, j * 128 : (j + 1) * 128]
                    corr[c, comp, x, y] = value
                    acc = packed(acc, value, comp * 16 + j)
            return acc

        zpack[1, c] = lax.fori_loop(0, comps, prolong, jnp.zeros((rows, 128), F32))
        send_faces(1, corr, c)
        send_x(1, corr, c, 0, AHEAD if c + 1 < CHUNKS else comps)

    for c in range(CHUNKS):

        def emit(b, value):
            out[pl.ds(c * rows * blocks + b, rows, stride=blocks), :] = value

        await_faces(1, c, (2, 3, 4, 5))
        interface_sum(1, corr, c, INNER, emit)
        await_faces(1, c, (0, 1))
        interface_sum(1, corr, c, OUTER, emit)

    for c in range(CHUNKS):
        drain_faces(0, field, c)
        drain_faces(1, corr, c)
        part_copy(c, 2, 0, False).wait_send()
        for a, b in NEAR:
            part_copy(c, a, b, False).wait_send()
            part_copy(c, a, b, True).wait_send()
    for a, b in FULL:
        index_copy(a, b).wait_send()


def per_device(
    residual,
    interface_scaling,
    primal_basis,
    primal_index,
    coarse_inverse,
    schur_tiles,
    tile_cols,
    tile_count,
    region_id,
    region_viscosity,
):
    rhs, comps, cells_x, cells_y, cells_z = residual.shape
    blocks = comps * cells_x * cells_y
    slots = schur_tiles.shape[4]
    primal = primal_basis.shape[3]
    coarse = coarse_inverse.shape[1]
    rows = rhs // CHUNKS
    sizes = (
        lax.axis_size("gx"),
        lax.axis_size("gy"),
        lax.axis_size("gz"),
        rhs,
        blocks,
        comps,
        slots,
    )
    face = pltpu.VMEM((2, CHUNKS, comps, cells_x, rows, cells_z), F32)
    ends = pltpu.VMEM((2, CHUNKS, rows, cells_z), F32)
    dma = pltpu.SemaphoreType.DMA
    hbm = pl.BlockSpec(memory_space=pltpu.HBM)
    operands = (
        residual.reshape(rhs * blocks, cells_z),
        interface_scaling.reshape(blocks, cells_z),
        primal_basis.reshape(primal, blocks * cells_z),
        primal_index.reshape(1, primal),
        coarse_inverse,
        schur_tiles.reshape(blocks, slots, cells_z, cells_z),
        tile_cols.transpose(0, 1, 4, 2, 3).reshape(slots, 1, blocks),
        tile_count.reshape(1, blocks),
        region_id,
        region_viscosity.reshape(1, -1),
    )
    operands = [
        v if v.size == 1 else pltpu.with_memory_space_constraint(v, pltpu.HBM) for v in operands
    ]
    out = pl.pallas_call(
        functools.partial(kernel, sizes),
        out_shape=jax.ShapeDtypeStruct((rhs * blocks, cells_z), F32),
        in_specs=[hbm] * 8 + [pl.BlockSpec(memory_space=pltpu.SMEM), hbm],
        out_specs=pl.BlockSpec(memory_space=pltpu.VMEM),
        scratch_shapes=[
            pltpu.SMEM((1, primal), jnp.int32),
            pltpu.SMEM((slots, 1, blocks), jnp.int32),
            pltpu.SMEM((1, blocks), jnp.int32),
            pltpu.SMEM((1, region_viscosity.shape[0]), F32),
            pltpu.VMEM((rhs * blocks, cells_z), F32),
            pltpu.VMEM((blocks, cells_z), F32),
            pltpu.VMEM((primal, blocks * cells_z), BF16),
            pltpu.VMEM((coarse, coarse), F32),
            pltpu.VMEM((blocks, slots, cells_z, cells_z), BF16),
            pltpu.VMEM((SLOTS, 1, primal), jnp.int32),
            pltpu.VMEM((CHUNKS, comps, cells_x, cells_y, rows, cells_z), F32),
            pltpu.VMEM((CHUNKS, blocks + 1, rows, cells_z), BF16),
            pltpu.VMEM((CHUNKS, comps, cells_x, cells_y, rows, cells_z), F32),
            ends,
            face,
            face,
            face,
            face,
            ends,
            ends,
            pltpu.VMEM((CHUNKS, SLOTS, rows, primal), F32),
            pltpu.VMEM((CHUNKS, rows, primal), F32),
            pltpu.VMEM((primal, coarse), F32),
            pltpu.VMEM((2 * primal, coarse), BF16),
            pltpu.VMEM((SLOTS, 2 * primal, primal), BF16),
            dma((9,)),
            dma((CHUNKS,)),
            dma((2, CHUNKS, 6)),
            dma((2, CHUNKS, 6)),
            dma((SLOTS,)),
            dma((SLOTS,)),
            dma((CHUNKS, SLOTS)),
            dma((CHUNKS, SLOTS)),
        ],
        compiler_params=pltpu.CompilerParams(
            collective_id=0, has_side_effects=True, vmem_limit_bytes=52 * 2**20
        ),
    )(*operands)
    return out.reshape(residual.shape)


def solution(mesh):
    in_specs = (
        P(None, None, "gx", "gy", "gz"),
        P(None, "gx", "gy", "gz"),
        P("gx", "gy", "gz", None, None),
        P("gx", "gy", "gz", None),
        P("gx", None),
        P("gx", "gy", "gz", None, None, None, None),
        P("gx", "gy", "gz", None, None),
        P("gx", "gy", "gz", None),
        P("gx", "gy", "gz"),
        P(),
    )
    out_specs = P(None, None, "gx", "gy", "gz")
    return jax.shard_map(
        per_device, mesh=mesh, in_specs=in_specs, out_specs=out_specs, check_vma=False
    )
```

```python
import functools
import math

import jax
import jax.numpy as jnp
from jax import lax
from jax.experimental import pallas as pl
from jax.experimental.pallas import tpu as pltpu
from jax.sharding import PartitionSpec as P

MESH = pl.DeviceIdType.MESH
CHUNKS = 2
RELAYED = ((1, 1),)
INNER = (1, 2)
OUTER = (0, 3)
GROUP_Y = 4
GROUP_Z = 4
SLOTS = GROUP_Y * GROUP_Z
NEAR = tuple((a, b) for a in range(2) for b in range(GROUP_Z) if (a, b) != (0, 0))
FULL = tuple((a, b) for a in range(GROUP_Y) for b in range(GROUP_Z) if (a, b) != (0, 0))
BF16 = jnp.bfloat16
F32 = jnp.float32
NT = (((1,), (1,)), ((), ()))


def flipped(gy, a):
    return (gy, gy + 1 - 2 * (gy % 2), (gy + 2) % 4, 3 - gy)[a]


def kernel(
    sizes,
    res_hbm,
    scale_hbm,
    basis_hbm,
    index_hbm,
    inverse_hbm,
    tiles_hbm,
    cols_hbm,
    count_hbm,
    region_smem,
    visc_hbm,
    out,
    index_smem,
    cols_smem,
    count_smem,
    visc_smem,
    lin,
    scale,
    basis,
    inverse,
    tiles,
    index_all,
    field,
    weighted,
    corr,
    zpack,
    x_low,
    x_high,
    y_low,
    y_high,
    z_low,
    z_high,
    relay,
    parts,
    part_own,
    picked_rows,
    split_rows,
    gathered,
    load_sem,
    in_sem,
    face_send,
    face_recv,
    index_send,
    index_recv,
    part_send,
    part_recv,
    relay_send,
    relay_recv,
):
    n_gx, n_gy, n_gz, rhs, blocks, comps, slots = sizes
    rows = rhs // CHUNKS
    gx, gy, gz = lax.axis_index("gx"), lax.axis_index("gy"), lax.axis_index("gz")

    sides = (
        (gx > 0, (gx - 1, gy, gz)),
        (gx < n_gx - 1, (gx + 1, gy, gz)),
        (gy > 0, (gx, gy - 1, gz)),
        (gy < n_gy - 1, (gx, gy + 1, gz)),
        (gz > 0, (gx, gy, gz - 1)),
        (gz < n_gz - 1, (gx, gy, gz + 1)),
    )

    def peer(a, b):
        return (gx, flipped(gy, a), (gz + b) % GROUP_Z)

    def load_chunk(c):
        span = pl.ds(c * rows * blocks, rows * blocks)
        return pltpu.make_async_copy(res_hbm.at[span], lin.at[span], in_sem.at[c])

    loads = (
        pltpu.make_async_copy(index_hbm, index_all.at[0], load_sem.at[0]),
        pltpu.make_async_copy(scale_hbm, scale, load_sem.at[1]),
        pltpu.make_async_copy(inverse_hbm, inverse, load_sem.at[2]),
        pltpu.make_async_copy(basis_hbm, basis, load_sem.at[3]),
        pltpu.make_async_copy(tiles_hbm, tiles, load_sem.at[4]),
        pltpu.make_async_copy(index_hbm, index_smem, load_sem.at[5]),
        pltpu.make_async_copy(cols_hbm, cols_smem, load_sem.at[6]),
        pltpu.make_async_copy(count_hbm, count_smem, load_sem.at[7]),
        pltpu.make_async_copy(visc_hbm, visc_smem, load_sem.at[8]),
    )
    for c in range(CHUNKS):
        load_chunk(c).start()
    loads[0].start()
    for copy in loads[5:]:
        copy.start()

    barrier = pltpu.get_barrier_semaphore()
    expected = 0
    two_off = (
        (gx > 1, (gx - 2, gy, gz)),
        (gx < n_gx - 2, (gx + 2, gy, gz)),
    )
    for there, device in sides + two_off:

        @pl.when(there)
        def _():
            pl.semaphore_signal(barrier, inc=1, device_id=device, device_id_type=MESH)

        expected = expected + there.astype(jnp.int32)
    for a, b in FULL:
        pl.semaphore_signal(barrier, inc=1, device_id=peer(a, b), device_id_type=MESH)

    def index_copy(a, b):
        k = a * GROUP_Z + b
        return pltpu.make_async_remote_copy(
            src_ref=index_all.at[0],
            dst_ref=index_all.at[k],
            send_sem=index_send.at[k],
            recv_sem=index_recv.at[k],
            device_id=peer(a, b),
            device_id_type=MESH,
        )

    lane = lax.broadcasted_iota(jnp.int32, (rows, 128), 1)

    def face_copies(phase, source, c):
        pairs = (
            (source.at[c, :, 0], x_high),
            (source.at[c, :, 3], x_low),
            (source.at[c, :, :, 0], y_high),
            (source.at[c, :, :, 3], y_low),
            (zpack.at[phase, c], z_high),
            (zpack.at[phase, c], z_low),
        )
        return [
            pltpu.make_async_remote_copy(
                src_ref=src,
                dst_ref=dst.at[phase, c],
                send_sem=face_send.at[phase, c, side],
                recv_sem=face_recv.at[phase, c, side ^ 1],
                device_id=sides[side][1],
                device_id_type=MESH,
            )
            for side, (src, dst) in enumerate(pairs)
        ]

    landing = (x_low, x_high, y_low, y_high, z_low, z_high)

    odd, level = gx % 2, gx // 2
    detour = odd * (level + 1) + (1 - odd) * (4 - level)
    passing = odd * level + (1 - odd) * (3 - level)

    def x_piece(phase, source, c, side, j):
        return pltpu.make_async_remote_copy(
            src_ref=source.at[c, :, 3 * side, j],
            dst_ref=(x_high, x_low)[side].at[phase, c, :, j],
            send_sem=face_send.at[phase, c, side],
            recv_sem=face_recv.at[phase, c, 1 - side],
            device_id=sides[side][1],
            device_id_type=MESH,
        )

    def x_detour(phase, source, c, side, j):
        return pltpu.make_async_remote_copy(
            src_ref=source.at[c, :, 3 * side, j],
            dst_ref=relay.at[phase, j],
            send_sem=face_send.at[phase, c, side],
            recv_sem=relay_recv.at[phase, j],
            device_id=two_off[side][1],
            device_id_type=MESH,
        )

    def x_onward(phase, c, side, j):
        return pltpu.make_async_remote_copy(
            src_ref=relay.at[phase, j],
            dst_ref=(x_low, x_high)[side].at[phase, c, :, j],
            send_sem=relay_send.at[phase, j],
            recv_sem=face_recv.at[phase, c, side],
            device_id=sides[side][1],
            device_id_type=MESH,
        )

    def send_onward(phase, c):
        for side in range(2):
            for j in range(3):

                @pl.when((odd == 1 - side) & (j < passing))
                def _():
                    pltpu.make_async_remote_copy(
                        src_ref=relay.at[phase, j],
                        dst_ref=relay.at[phase, j],
                        send_sem=relay_send.at[phase, j],
                        recv_sem=relay_recv.at[phase, j],
                        device_id=sides[side][1],
                        device_id_type=MESH,
                    ).wait_recv()
                    x_onward(phase, c, side, j).start()

    def drain_onward(phase, c):
        for side in range(2):
            for j in range(3):

                @pl.when((odd == 1 - side) & (j < passing))
                def _():
                    x_onward(phase, c, side, j).wait_send()

    def send_faces(phase, source, c):
        for side in (4, 5, 2, 3):

            @pl.when(sides[side][0])
            def _():
                face_copies(phase, source, c)[side].start()

    def send_x(phase, source, c):
        copies = face_copies(phase, source, c)
        relayed = (phase, c) in RELAYED
        for side in range(2):

            @pl.when(sides[side][0] & (odd != side) if relayed else sides[side][0])
            def _():
                copies[side].start()

        if relayed:
            for side in range(2):
                for j in range(4):
                    if j < 3:

                        @pl.when(sides[side][0] & (odd == side) & (j < detour))
                        def _():
                            x_detour(phase, source, c, side, j).start()

                    @pl.when(sides[side][0] & (odd == side) & (j >= detour))
                    def _():
                        x_piece(phase, source, c, side, j).start()

    def await_faces(phase, c, chosen):
        for side in chosen:
            land = landing[side].at[phase, c]
            arrived = pltpu.make_async_remote_copy(
                src_ref=land,
                dst_ref=land,
                send_sem=face_send.at[phase, c, side],
                recv_sem=face_recv.at[phase, c, side],
                device_id=sides[side][1],
                device_id_type=MESH,
            )

            @pl.when(sides[side][0])
            def _():
                arrived.wait_recv()

    def drain_faces(phase, source, c):
        for side, copy in enumerate(face_copies(phase, source, c)):

            @pl.when(sides[side][0])
            def _():
                copy.wait_send()

    def packed(acc, value, b):
        return jnp.where(lane // 2 == b, pltpu.roll(value, 2 * b + 1, 1), acc)

    def pack_first(c):
        def body(comp, acc):
            for x in range(4):
                for y in range(4):
                    b = comp * 16 + x * 4 + y
                    value = lin[pl.ds(c * rows * blocks + b, rows, stride=blocks), :]
                    field[c, comp, x, y] = value
                    acc = packed(acc, value, b)
            return acc

        zpack[0, c] = lax.fori_loop(0, comps, body, jnp.zeros((rows, 128), F32))

    def interface_sum(phase, source, c, planes, emit):
        low = pltpu.roll(z_low[phase, c], 1, 1)
        high = pltpu.roll(z_high[phase, c], 127, 1)
        ends = jnp.where(lane % 2 == 1, low, high)
        edge = (lane == 0) | (lane == 127)

        def body(comp, carry):
            for x in planes:
                for y in range(4):
                    b = comp * 16 + x * 4 + y
                    total = source[c, comp, x, y]
                    total = total + jnp.where(edge, pltpu.roll(ends, 127 - 2 * b, 1), 0.0)
                    if x == 0:
                        total = total + x_low[phase, c, comp, y]
                    if x == 3:
                        total = total + x_high[phase, c, comp, y]
                    if y == 0:
                        total = total + y_low[phase, c, comp, x]
                    if y == 3:
                        total = total + y_high[phase, c, comp, x]
                    emit(b, total * scale[pl.ds(b, 1), :])
            return carry

        lax.fori_loop(0, comps, body, 0)

    load_chunk(0).wait()
    pack_first(0)
    loads[2].start()
    loads[0].wait()
    pl.semaphore_wait(barrier, expected + len(FULL))
    for a, b in FULL:
        index_copy(a, b).start()
    send_faces(0, field, 0)
    send_x(0, field, 0)
    for c in range(1, CHUNKS):
        load_chunk(c).wait()
        pack_first(c)
        send_faces(0, field, c)

    for k in (1, 3, 4):
        loads[k].start()

    for side in range(6):

        @pl.when(jnp.logical_not(sides[side][0]))
        def _():
            landing[side][...] = jnp.zeros_like(landing[side])


    if (0, 0) in RELAYED:
        send_onward(0, 0)
    for copy in loads[5:]:
        copy.wait()

    loads[2].wait()

    def pick_row(p, carry):
        picked_rows[pl.ds(p, 1), :] = inverse[pl.ds(index_smem[0, p], 1), :]
        return carry

    lax.fori_loop(0, 128, pick_row, 0, unroll=8)
    rows_f32 = picked_rows[...]
    high_part = rows_f32.astype(BF16)
    split_rows[0:128, :] = high_part
    split_rows[128:256, :] = (rows_f32 - high_part.astype(F32)).astype(BF16)

    for a, b in FULL:
        index_copy(a, b).wait_recv()

    def pick_columns(k, carry):
        coarse = split_rows.shape[1]
        ids = lax.broadcasted_iota(jnp.int32, (coarse, 128), 0)
        one_hot = jnp.where(ids == index_all[k], 1.0, 0.0).astype(BF16)
        found = jnp.dot(split_rows[...], one_hot, preferred_element_type=F32).astype(BF16)
        gathered[k] = found
        return carry

    lax.fori_loop(0, SLOTS, pick_columns, 0)

    def part_copy(c, a, b, forward):
        slot = (a + 2) * GROUP_Z + b if forward else a * GROUP_Z + b
        return pltpu.make_async_remote_copy(
            src_ref=parts.at[c, 2 * GROUP_Z] if forward else part_own.at[c],
            dst_ref=parts.at[c, slot],
            send_sem=part_send.at[c, slot],
            recv_sem=part_recv.at[c, slot],
            device_id=peer(a, b),
            device_id_type=MESH,
        )

    loads[1].wait()
    loads[3].wait()
    visc = jnp.full((rows, 128), visc_smem[0, region_smem[0, 0, 0]], F32)
    inv_visc = 1.0 / visc
    coarse_scale = math.sqrt(blocks * 128 / 128)

    for c in range(CHUNKS):
        def keep(b, value):
            weighted[c, b] = value.astype(BF16)

        def restrict(planes):
            def body(comp, acc):
                picks = [weighted[c, comp * 16 + x * 4 + y] for x in planes for y in range(4)]
                spans = [
                    basis[:, pl.ds(pl.multiple_of(comp * 2048 + x * 512, 512), 512)] for x in planes
                ]
                return acc + lax.dot_general(
                    jnp.concatenate(picks, axis=1),
                    jnp.concatenate(spans, axis=1),
                    NT,
                    preferred_element_type=F32,
                )

            return body

        await_faces(0, c, (2, 3, 4, 5))
        interface_sum(0, field, c, INNER, keep)
        part = lax.fori_loop(0, comps, restrict(INNER), jnp.zeros((rows, 128), F32))
        await_faces(0, c, (0, 1))
        interface_sum(0, field, c, OUTER, keep)
        weighted[c, blocks] = jnp.zeros((rows, 128), BF16)
        part = lax.fori_loop(0, comps, restrict(OUTER), part)
        part_own[c] = part
        parts[c, 0] = part
        part_copy(c, 2, 0, False).start()
        for a, b in NEAR:
            part_copy(c, a, b, False).start()
        if c > 0:
            send_x(1, corr, c - 1)
        if c + 1 < CHUNKS:
            send_x(0, field, c + 1)
        if c == 0:
            loads[4].wait()

        def schur_row(r, carry):
            picks = [
                weighted[c, jnp.where(k < count_smem[0, r], cols_smem[k, 0, r], blocks)]
                for k in range(slots)
            ]
            lhs = jnp.concatenate(picks, axis=1)
            tile = jnp.concatenate([tiles[r, k] for k in range(slots)], axis=1)
            product = lax.dot_general(lhs, tile, NT, preferred_element_type=F32)
            corr[c, r // 16, (r // 4) % 4, r % 4] = product * inv_visc
            return carry

        lax.fori_loop(0, 12, schur_row, 0, unroll=2)
        part_copy(c, 2, 0, False).wait_recv()
        for a, b in NEAR:
            part_copy(c, a, b, True).start()
        lax.fori_loop(12, blocks, schur_row, 0, unroll=2)
        for a, b in NEAR:
            part_copy(c, a, b, False).wait_recv()
            part_copy(c, a, b, True).wait_recv()

        everyone = jnp.concatenate([parts[c, k] for k in range(SLOTS)], axis=1)
        top = everyone.astype(BF16)
        rest = (everyone - top.astype(F32)).astype(BF16)
        inv_high = jnp.concatenate([gathered[k, 0:128] for k in range(SLOTS)], axis=1)
        inv_low = jnp.concatenate([gathered[k, 128:256] for k in range(SLOTS)], axis=1)
        local = lax.dot_general(top, inv_high, NT, preferred_element_type=F32)
        local = local + lax.dot_general(rest, inv_high, NT, preferred_element_type=F32)
        local = local + lax.dot_general(top, inv_low, NT, preferred_element_type=F32)
        local = local.astype(BF16)

        def prolong(comp, acc):
            rhs_part = basis[:, pl.ds(pl.multiple_of(comp * 2048, 2048), 2048)]
            fix = jnp.dot(local, rhs_part, preferred_element_type=F32) * coarse_scale
            for x in range(4):
                for y in range(4):
                    j = x * 4 + y
                    value = corr[c, comp, x, y] + fix[:, j * 128 : (j + 1) * 128]
                    corr[c, comp, x, y] = value
                    acc = packed(acc, value, comp * 16 + j)
            return acc

        zpack[1, c] = lax.fori_loop(0, comps, prolong, jnp.zeros((rows, 128), F32))
        send_faces(1, corr, c)
        if c + 1 == CHUNKS:
            send_x(1, corr, c)

    for c in range(CHUNKS):

        def emit(b, value):
            out[pl.ds(c * rows * blocks + b, rows, stride=blocks), :] = value

        if c == 0 and (1, 1) in RELAYED:
            send_onward(1, 1)
        await_faces(1, c, (2, 3, 4, 5))
        interface_sum(1, corr, c, INNER, emit)
        await_faces(1, c, (0, 1))
        interface_sum(1, corr, c, OUTER, emit)

    for c in range(CHUNKS):
        drain_faces(0, field, c)
        drain_faces(1, corr, c)
        part_copy(c, 2, 0, False).wait_send()
        for a, b in NEAR:
            part_copy(c, a, b, False).wait_send()
            part_copy(c, a, b, True).wait_send()
    for phase, c in RELAYED:
        drain_onward(phase, c)
    for a, b in FULL:
        index_copy(a, b).wait_send()


def per_device(
    residual,
    interface_scaling,
    primal_basis,
    primal_index,
    coarse_inverse,
    schur_tiles,
    tile_cols,
    tile_count,
    region_id,
    region_viscosity,
):
    rhs, comps, cells_x, cells_y, cells_z = residual.shape
    blocks = comps * cells_x * cells_y
    slots = schur_tiles.shape[4]
    primal = primal_basis.shape[3]
    coarse = coarse_inverse.shape[1]
    rows = rhs // CHUNKS
    sizes = (
        lax.axis_size("gx"),
        lax.axis_size("gy"),
        lax.axis_size("gz"),
        rhs,
        blocks,
        comps,
        slots,
    )
    face = pltpu.VMEM((2, CHUNKS, comps, cells_x, rows, cells_z), F32)
    ends = pltpu.VMEM((2, CHUNKS, rows, cells_z), F32)
    dma = pltpu.SemaphoreType.DMA
    hbm = pl.BlockSpec(memory_space=pltpu.HBM)
    operands = (
        residual.reshape(rhs * blocks, cells_z),
        interface_scaling.reshape(blocks, cells_z),
        primal_basis.reshape(primal, blocks * cells_z),
        primal_index.reshape(1, primal),
        coarse_inverse,
        schur_tiles.reshape(blocks, slots, cells_z, cells_z),
        tile_cols.transpose(0, 1, 4, 2, 3).reshape(slots, 1, blocks),
        tile_count.reshape(1, blocks),
        region_id,
        region_viscosity.reshape(1, -1),
    )
    operands = [
        v if v.size == 1 else pltpu.with_memory_space_constraint(v, pltpu.HBM) for v in operands
    ]
    out = pl.pallas_call(
        functools.partial(kernel, sizes),
        out_shape=jax.ShapeDtypeStruct((rhs * blocks, cells_z), F32),
        in_specs=[hbm] * 8 + [pl.BlockSpec(memory_space=pltpu.SMEM), hbm],
        out_specs=pl.BlockSpec(memory_space=pltpu.VMEM),
        scratch_shapes=[
            pltpu.SMEM((1, primal), jnp.int32),
            pltpu.SMEM((slots, 1, blocks), jnp.int32),
            pltpu.SMEM((1, blocks), jnp.int32),
            pltpu.SMEM((1, region_viscosity.shape[0]), F32),
            pltpu.VMEM((rhs * blocks, cells_z), F32),
            pltpu.VMEM((blocks, cells_z), F32),
            pltpu.VMEM((primal, blocks * cells_z), BF16),
            pltpu.VMEM((coarse, coarse), F32),
            pltpu.VMEM((blocks, slots, cells_z, cells_z), BF16),
            pltpu.VMEM((SLOTS, 1, primal), jnp.int32),
            pltpu.VMEM((CHUNKS, comps, cells_x, cells_y, rows, cells_z), F32),
            pltpu.VMEM((CHUNKS, blocks + 1, rows, cells_z), BF16),
            pltpu.VMEM((CHUNKS, comps, cells_x, cells_y, rows, cells_z), F32),
            ends,
            face,
            face,
            face,
            face,
            ends,
            ends,
            pltpu.VMEM((2, 3, comps, rows, cells_z), F32),
            pltpu.VMEM((CHUNKS, SLOTS, rows, primal), F32),
            pltpu.VMEM((CHUNKS, rows, primal), F32),
            pltpu.VMEM((primal, coarse), F32),
            pltpu.VMEM((2 * primal, coarse), BF16),
            pltpu.VMEM((SLOTS, 2 * primal, primal), BF16),
            dma((9,)),
            dma((CHUNKS,)),
            dma((2, CHUNKS, 6)),
            dma((2, CHUNKS, 6)),
            dma((SLOTS,)),
            dma((SLOTS,)),
            dma((CHUNKS, SLOTS)),
            dma((CHUNKS, SLOTS)),
            dma((2, 3)),
            dma((2, 3)),
        ],
        compiler_params=pltpu.CompilerParams(
            collective_id=0, has_side_effects=True, vmem_limit_bytes=52 * 2**20
        ),
    )(*operands)
    return out.reshape(residual.shape)


def solution(mesh):
    in_specs = (
        P(None, None, "gx", "gy", "gz"),
        P(None, "gx", "gy", "gz"),
        P("gx", "gy", "gz", None, None),
        P("gx", "gy", "gz", None),
        P("gx", None),
        P("gx", "gy", "gz", None, None, None, None),
        P("gx", "gy", "gz", None, None),
        P("gx", "gy", "gz", None),
        P("gx", "gy", "gz"),
        P(),
    )
    out_specs = P(None, None, "gx", "gy", "gz")
    return jax.shard_map(
        per_device, mesh=mesh, in_specs=in_specs, out_specs=out_specs, check_vma=False
    )
```
